512 devices in a mesh: section: 4 (over x), frame: 16 (over y_lo, z), chan: 8 (over y_hi, core).
Axes of the slice: x: 4, y: 8 (y_hi: 4, y_lo: 2; y = y_hi * 2 + y_lo), z: 8, core: 2. Of those that a mesh axis runs over, the one named last changes fastest.
Arguments:
- upstream: bfloat16 [512, 8, 16, 128], P('chan', None, 'frame'), may hold values from -6 to 6
- acts: bfloat16 [4, 512, 8, 16, 128], P('section', None, None, 'frame'), may hold values from -6 to 6
- weights: bfloat16 [4, 27, 512, 512], P('section', None, 'chan'), may hold values from -0.0625 to 0.0625
Outputs:
- grads: bfloat16 [4, 512, 8, 16, 128], P('section', 'chan', None, 'frame')
- weight_grads: bfloat16 [4, 27, 512, 512], P('section', None, 'chan')
The draws below stay inside these ranges and needn't reach their ends.
All inputs are finite; a program needn't handle non-finite values.
Results may differ from the reference program's by a relative error of at most 0.03.
Values may be sent and summed in bfloat16 or wider, within the bound.
A program may use at most 64 MiB of HBM per device.

```python
import jax
import jax.numpy as jnp

C = 512
WIDTH = 128
LAYERS = 4
FRAMES = 8
ROWS = 16
N_SECTION = 4


def strengthened(entries, key, source, target, blocks, factor):
    def block_of(dim):
        return (jnp.arange(entries.shape[dim]) // (entries.shape[dim] // blocks)).reshape((-1,) + (1,) * (entries.ndim - 1 - dim))

    first = jax.random.permutation(key, blocks)[block_of(target)]
    second = (block_of(target) + blocks // 2) % blocks
    return jnp.where((block_of(source) == first) | (block_of(source) == second), factor * entries, entries)


def steps_of(stream_key, shape, cuts, low, top_value):
    def one(position, blocks):
        draws = jax.random.uniform(jax.random.fold_in(jax.random.fold_in(stream_key, 6), position), (blocks,), jnp.float32, low / len(cuts), top_value / len(cuts))
        return jnp.repeat(jnp.exp(draws), shape[position] // blocks).reshape((-1,) + (1,) * (len(shape) - position - 1))

    loudness = one(*cuts[0])
    for cut in cuts[1:]:
        loudness = loudness * one(*cut)
    return loudness


def gaussian(stream_key, dims, scale, reach, split=(), held_as=jnp.bfloat16):
    entries = scale * jax.random.normal(stream_key, dims, jnp.float32)
    if split:
        entries = entries * steps_of(stream_key, dims, split, -0.22, 0.18)
    return jnp.clip(entries, -reach, reach).astype(held_as)


def noise_with(key, dims, scale, bound, cuts, heavy, held_as=jnp.bfloat16):
    entries = scale * jax.random.normal(key, dims, jnp.float32)
    if cuts:
        entries = entries * steps_of(key, dims, cuts, -0.22, 0.18)
    return jnp.clip(strengthened(entries, jax.random.fold_in(key, 3), *heavy), -bound, bound).astype(held_as)


def setup_inputs(seed: int = 0) -> dict:
    key_of = jax.random.split(jax.random.key(seed), 4)
    return {
        "upstream": gaussian(key_of[0], (C, FRAMES, ROWS, WIDTH), 1.0, 6.0, ((0, 8), (2, 16))),
        "acts": gaussian(key_of[1], (LAYERS, C, FRAMES, ROWS, WIDTH), 1.0, 6.0, ((0, 4), (3, 16))),
        "weights": noise_with(key_of[2], (LAYERS, 27, C, C), (27 * C) ** -0.5, 0.0625, ((0, 4), (2, 8)), (2, 3, 8, 2.0)),
    }


def shifted_list(gradient):
    frames_n, rows_n, width_n = gradient.shape[1], gradient.shape[2], gradient.shape[3]
    padded = jnp.pad(gradient, ((0, 0), (0, 2), (1, 1), (1, 1)))
    pieces = []
    for t_lag in range(3):
        for r_off in (-1, 0, 1):
            for w_off in (-1, 0, 1):
                pieces.append(padded[:, t_lag:t_lag + frames_n, 1 - r_off:1 - r_off + rows_n, 1 - w_off:1 - w_off + width_n])
    return pieces


def reference(upstream, acts, weights):
    gradient = upstream
    results = []
    kernels = []
    for layer_index in range(N_SECTION):
        stored = acts[layer_index].astype(jnp.float32)
        logistic = jax.nn.sigmoid(stored)
        slopes = logistic * (1.0 + stored * (1.0 - logistic))
        features = (stored * logistic).astype(jnp.bfloat16).reshape(C, -1)
        transposed = jnp.zeros((C, features.shape[1]), jnp.float32)
        tap_grads = []
        for tap_index, shifted in enumerate(shifted_list(gradient)):
            flat = shifted.reshape(C, -1)
            transposed = transposed + jnp.dot(weights[layer_index, tap_index].T, flat, preferred_element_type=jnp.float32)
            tap_grads.append(jnp.dot(flat, features.T, preferred_element_type=jnp.float32))
        gradient = (gradient.astype(jnp.float32) + slopes * transposed.reshape(gradient.shape)).astype(jnp.bfloat16)
        results.append(gradient)
        kernels.append(jnp.stack(tap_grads).astype(jnp.bfloat16))
    return jnp.stack(results), jnp.stack(kernels)
```

```python
import functools

import jax
import jax.numpy as jnp
from jax import lax
from jax.experimental import pallas as pl
from jax.experimental.pallas import tpu as pltpu
from jax.sharding import PartitionSpec as P

MESH = pl.DeviceIdType.MESH
BLOCK = 2
GROUP = 64
SLAB = 9 * GROUP
DEPTH = 27 * GROUP
PADDED = 28 * GROUP


def remote(src, dst, send_sem, recv_sem, device):
    return pltpu.make_async_remote_copy(
        src_ref=src, dst_ref=dst, send_sem=send_sem, recv_sem=recv_sem, device_id=device, device_id_type=MESH
    )


def pipeline_kernel(
    sections, rows, chips, frames,
    up_ref, acts_ref, w_ref, grads_ref, wg_ref,
    g_own, g_par, x_own, x_par, wt, wp, part, recv, a32, slope, feat, acc, o32, gout,
    u_send, g_send, g_recv, f_send, f_recv, r_send, r_recv, w_send, w_recv,
):
    channels = w_ref.shape[1]
    chans = 2 * chips
    blocks = frames // BLOCK
    width = 128
    s = lax.axis_index("section")
    f = lax.axis_index("frame")
    d = lax.axis_index("chan")
    chip = d // 2
    core = d % 2
    partner = d + 1 - 2 * core

    barrier = pltpu.get_barrier_semaphore()
    peers = []
    for ds in (1, sections - 1):
        for df in (0, 1, rows - 1):
            peers.append(((s + ds) % sections, (f + df) % rows, d))
    for df in (1, rows - 1):
        peers.append((s, (f + df) % rows, d))
    peers.append((s, f, partner))
    for dq in range(1, chips):
        peers.append((s, f, ((chip + dq) % chips) * 2 + core))
    for peer in peers:
        pl.semaphore_signal(barrier, inc=1, device_id=peer, device_id_type=MESH)

    has_up = f > 0
    has_down = f < rows - 1

    for g in (g_own, g_par):
        for row in range(3):
            g[row, frames:] = jnp.zeros((2, GROUP, width), jnp.bfloat16)

        @pl.when(jnp.logical_not(has_down))
        def _():
            g[0, :frames] = jnp.zeros((frames, GROUP, width), jnp.bfloat16)

        @pl.when(jnp.logical_not(has_up))
        def _():
            g[2, :frames] = jnp.zeros((frames, GROUP, width), jnp.bfloat16)

    for x in (x_own, x_par):
        x[frames * SLAB :] = jnp.zeros((x.shape[0] - frames * SLAB, width), jnp.bfloat16)

    @pl.when(s == 0)
    def _():
        o32[...] = up_ref[...].astype(jnp.float32)
        for t in range(frames):
            g_own[1, t] = o32[pl.ds(t, GROUP, stride=frames), :].astype(jnp.bfloat16)

    for q in range(chans):
        wt[q, :, DEPTH:] = jnp.zeros((GROUP, PADDED - DEPTH), jnp.bfloat16)
    step = 2 * GROUP
    for k in range(0, DEPTH, step):
        size = min(step, DEPTH - k)
        turned = w_ref[k : k + size, :].astype(jnp.float32).T.astype(jnp.bfloat16)
        for q in range(chans):
            wt[q, :, k : k + size] = turned[q * GROUP : (q + 1) * GROUP]

    pl.semaphore_wait(barrier, len(peers))

    def frames_of(b):
        return (blocks - 1 - b) * BLOCK

    def weight_copy(q):
        return remote(wt.at[2 * q + 1 - core], wp.at[q], w_send.at[q], w_recv.at[q], (s, f, partner))

    def row_copy(src, b, slot, section, row, out_sem=g_send):
        first = frames_of(b)
        return remote(
            src,
            g_own.at[slot, pl.ds(first, BLOCK)],
            out_sem.at[b, slot],
            g_recv.at[b, slot],
            (section, row, d),
        )

    def spread(src, b, section, centre, go):
        out_sem = g_send if centre else u_send
        if centre:
            go(row_copy(src, b, 1, section, f, out_sem))

        @pl.when(has_down)
        def _():
            go(row_copy(src, b, 2, section, (f + 1) % rows, out_sem))

        @pl.when(has_up)
        def _():
            go(row_copy(src, b, 0, section, (f + rows - 1) % rows, out_sem))

    def begin(copy):
        copy.start()

    def sent(copy):
        copy.wait_send()

    def arrived(copy):
        copy.wait_recv()

    def block_of(g, b):
        return g.at[1, pl.ds(frames_of(b), BLOCK)]

    for q in range(chips):
        weight_copy(q).start()

    @pl.when(s == 0)
    def _():
        for b in range(blocks):
            spread(block_of(g_own, b), b, s, False, begin)

    def forward_copy(b, slot):
        first = pl.ds(frames_of(b), BLOCK)
        return remote(
            g_own.at[slot, first], g_par.at[slot, first], f_send.at[b, slot], f_recv.at[b, slot], (s, f, partner)
        )

    def per_slot(fn):
        fn(1)
        pl.when(has_down)(lambda: fn(0))
        pl.when(has_up)(lambda: fn(2))

    def take(b):
        def one(slot):
            copy = row_copy(block_of(g_own, b), b, slot, s, f)
            if slot == 1:
                pl.when(s > 0)(lambda: copy.wait_recv())
            else:
                copy.wait_recv()
            forward_copy(b, slot).start()

        per_slot(one)

    lane = lax.broadcasted_iota(jnp.int32, (GROUP, width), 1)

    def build(g, x, t):
        for slot in range(3):
            row = g[slot, t].astype(jnp.float32)
            after = jnp.where(lane == width - 1, 0.0, pltpu.roll(row, width - 1, 1))
            before = jnp.where(lane == 0, 0.0, pltpu.roll(row, 1, 1))
            base = t * SLAB + slot * 3 * GROUP
            x[base : base + GROUP] = after.astype(jnp.bfloat16)
            x[base + GROUP : base + 2 * GROUP] = row.astype(jnp.bfloat16)
            x[base + 2 * GROUP : base + 3 * GROUP] = before.astype(jnp.bfloat16)

    def columns(x, b):
        first = frames_of(b)
        return jnp.concatenate(
            [x[t * SLAB : t * SLAB + PADDED] for t in range(first, first + BLOCK)], axis=1
        )

    def term_copy(b, q):
        return remote(
            part.at[b, q], recv.at[b, chip], r_send.at[b, q], r_recv.at[b, chip], (s, f, 2 * q + core)
        )

    def term_arrival(b, q):
        return remote(
            part.at[b, q], recv.at[b, q], r_send.at[b, q], r_recv.at[b, q], (s, f, 2 * q + core)
        )

    hops = sorted(range(1, chips), key=lambda o: -min(o, chips - o))

    for b in range(blocks):
        first = frames_of(b)
        take(b)
        for t in range(first, first + BLOCK):
            build(g_own, x_own, t)
        lhs = jnp.concatenate([wt[2 * q + core] for q in range(chips)], axis=0)
        total = jnp.dot(lhs, columns(x_own, b), preferred_element_type=jnp.float32)
        if b == 0:
            for q in range(chips):
                weight_copy(q).wait_recv()
        per_slot(lambda slot: forward_copy(b, slot).wait_recv())
        for t in range(first, first + BLOCK):
            build(g_par, x_par, t)
        lhs = jnp.concatenate([wp[q] for q in range(chips)], axis=0)
        total = total + jnp.dot(lhs, columns(x_par, b), preferred_element_type=jnp.float32)
        for q in range(chips):
            part[b, q] = total[q * GROUP : (q + 1) * GROUP].astype(jnp.bfloat16)
        for o in hops:
            term_copy(b, (chip + o) % chips).start()

        if b == 0:
            a32[...] = acts_ref[...].astype(jnp.float32)
            for t in range(frames):
                own = a32[pl.ds(d * (GROUP * frames) + t, GROUP, stride=frames), :]
                logistic = 1.0 / (1.0 + jnp.exp(-own))
                slope[t] = logistic * (1.0 + own * (1.0 - logistic))
                for q in range(0, channels, step):
                    values = a32[pl.ds(q * frames + t, step, stride=frames), :]
                    values = values / (1.0 + jnp.exp(-values))
                    feat[t * width : (t + 1) * width, q : q + step] = values.T.astype(jnp.bfloat16)

        cells = slice(first * width, (first + BLOCK) * width)
        for k in range(3):
            lhs = jnp.concatenate(
                [x_own[(t + k) * SLAB : (t + k + 1) * SLAB] for t in range(first, first + BLOCK)], axis=1
            )
            add = jnp.dot(lhs, feat[cells, :], preferred_element_type=jnp.float32)
            at = slice(k * SLAB, (k + 1) * SLAB)
            if b > 0:
                add = add + acc[at]
            if b == blocks - 1:
                wg_ref[at] = add.astype(jnp.bfloat16)
            else:
                acc[at] = add

        back = part[b, chip].astype(jnp.float32)
        for o in reversed(hops):
            q = (chip + o) % chips
            term_arrival(b, q).wait_recv()
            back = back + recv[b, q].astype(jnp.float32)
        for n, t in enumerate(range(first, first + BLOCK)):
            new = g_own[1, t].astype(jnp.float32) + slope[t] * back[:, n * width : (n + 1) * width]
            new = new.astype(jnp.bfloat16)
            gout[t] = new
            o32[pl.ds(t, GROUP, stride=frames), :] = new.astype(jnp.float32)

        @pl.when(s < sections - 1)
        def _():
            spread(gout.at[pl.ds(first, BLOCK)], b, (s + 1) % sections, True, begin)

    grads_ref[...] = o32[...].astype(jnp.bfloat16)

    for q in range(chips):
        weight_copy(q).wait_send()

    @pl.when(s == 0)
    def _():
        for b in range(blocks):
            spread(block_of(g_own, b), b, s, False, sent)

    for b in range(blocks):
        per_slot(lambda slot: forward_copy(b, slot).wait_send())
        for o in hops:
            term_copy(b, (chip + o) % chips).wait_send()

    pl.when(s < sections - 1)(
        lambda: [
            spread(gout.at[pl.ds(frames_of(b), BLOCK)], b, (s + 1) % sections, True, sent) for b in range(blocks)
        ] and None
    )


def pipeline(sections, rows, chips, frames, upstream, acts, weights):
    channels = weights.shape[1]
    width = 128
    blocks = frames // BLOCK
    bf16, f32 = jnp.bfloat16, jnp.float32
    dma = pltpu.SemaphoreType.DMA
    vmem = pl.BlockSpec(memory_space=pltpu.VMEM)
    depth = (frames + 2) * SLAB + GROUP
    return pl.pallas_call(
        functools.partial(pipeline_kernel, sections, rows, chips, frames),
        out_shape=(
            jax.ShapeDtypeStruct((GROUP * frames, width), bf16),
            jax.ShapeDtypeStruct((DEPTH, channels), bf16),
        ),
        in_specs=[vmem] * 3,
        out_specs=(vmem, vmem),
        scratch_shapes=[
            pltpu.VMEM((3, frames + 2, GROUP, width), bf16),
            pltpu.VMEM((3, frames + 2, GROUP, width), bf16),
            pltpu.VMEM((depth, width), bf16),
            pltpu.VMEM((depth, width), bf16),
            pltpu.VMEM((2 * chips, GROUP, PADDED), bf16),
            pltpu.VMEM((chips, GROUP, PADDED), bf16),
            pltpu.VMEM((blocks, chips, GROUP, BLOCK * width), bf16),
            pltpu.VMEM((blocks, chips, GROUP, BLOCK * width), bf16),
            pltpu.VMEM((channels * frames, width), f32),
            pltpu.VMEM((frames, GROUP, width), f32),
            pltpu.VMEM((frames * width, channels), bf16),
            pltpu.VMEM((DEPTH, channels), f32),
            pltpu.VMEM((GROUP * frames, width), f32),
            pltpu.VMEM((frames, GROUP, width), bf16),
            dma((blocks, 3)),
            dma((blocks, 3)),
            dma((blocks, 3)),
            dma((blocks, 3)),
            dma((blocks, 3)),
            dma((blocks, chips)),
            dma((blocks, chips)),
            dma((chips,)),
            dma((chips,)),
        ],
        compiler_params=pltpu.CompilerParams(collective_id=0, has_side_effects=True),
        name="pipeline",
    )(upstream, acts, weights)


def solution(mesh):
    sections, rows, chans = (mesh.shape[a] for a in ("section", "frame", "chan"))

    def body(upstream, acts, weights):
        group, frames, _, width = upstream.shape
        channels = acts.shape[1]
        grads, kernel_sum = pipeline(
            sections,
            rows,
            chans // 2,
            frames,
            upstream.reshape(group * frames, width),
            acts.reshape(channels * frames, width),
            weights.reshape(27 * group, channels),
        )
        kernel_total = lax.psum(kernel_sum, "frame")
        return grads.reshape(1, group, frames, 1, width), kernel_total.reshape(1, 27, group, channels)

    return jax.shard_map(
        body,
        mesh=mesh,
        in_specs=(
            P("chan", None, "frame", None),
            P("section", None, None, "frame", None),
            P("section", None, "chan", None),
        ),
        out_specs=(P("section", "chan", None, "frame", None), P("section", None, "chan", None)),
        check_vma=False,
    )
```

```python
import functools

import jax
import jax.numpy as jnp
from jax import lax
from jax.experimental import pallas as pl
from jax.experimental.pallas import tpu as pltpu
from jax.sharding import PartitionSpec as P

MESH = pl.DeviceIdType.MESH
BLOCK = 2
GROUP = 64
SLAB = 9 * GROUP
DEPTH = 27 * GROUP
PADDED = 28 * GROUP


def remote(src, dst, send_sem, recv_sem, device):
    return pltpu.make_async_remote_copy(
        src_ref=src, dst_ref=dst, send_sem=send_sem, recv_sem=recv_sem, device_id=device, device_id_type=MESH
    )


def pipeline_kernel(
    sections, rows, chips, frames,
    up_ref, acts_ref, w_ref, grads_ref, wg_ref,
    g_own, g_par, x_own, x_par, wt, wp, part, recv, a32, slope, feat, acc, o32, gout,
    wsum, wfin, chain, short_chain, half_sum, half_in, whole_in,
    u_send, g_send, g_recv, f_send, f_recv, r_send, r_recv, w_send, w_recv,
    c_send, c_recv, y_send, y_recv, a_send, a_recv, b_send, b_recv, e_send, e_recv,
):
    channels = w_ref.shape[1]
    chans = 2 * chips
    blocks = frames // BLOCK
    width = 128
    s = lax.axis_index("section")
    f = lax.axis_index("frame")
    d = lax.axis_index("chan")
    chip = d // 2
    core = d % 2
    partner = d + 1 - 2 * core

    barrier = pltpu.get_barrier_semaphore()
    peers = []
    for ds in (1, sections - 1):
        for df in (0, 1, rows - 1):
            peers.append(((s + ds) % sections, (f + df) % rows, d))
    for df in (1, rows - 1):
        peers.append((s, (f + df) % rows, d))
    peers.append((s, f, partner))
    for dq in range(1, chips):
        peers.append((s, f, ((chip + dq) % chips) * 2 + core))
    ring = rows // 2
    lanes = ring // 2
    reach = ring // 2
    h = f // ring
    z = f % ring
    across = (s, (1 - h) * ring + z, d)
    peers.append(across)
    for dz in (1, ring - 1):
        peers.append((s, h * ring + (z + dz) % ring, d))
    for peer in peers:
        pl.semaphore_signal(barrier, inc=1, device_id=peer, device_id_type=MESH)

    has_up = f > 0
    has_down = f < rows - 1

    for g in (g_own, g_par):
        for row in range(3):
            g[row, frames:] = jnp.zeros((2, GROUP, width), jnp.bfloat16)

        @pl.when(jnp.logical_not(has_down))
        def _():
            g[0, :frames] = jnp.zeros((frames, GROUP, width), jnp.bfloat16)

        @pl.when(jnp.logical_not(has_up))
        def _():
            g[2, :frames] = jnp.zeros((frames, GROUP, width), jnp.bfloat16)

    for x in (x_own, x_par):
        x[frames * SLAB :] = jnp.zeros((x.shape[0] - frames * SLAB, width), jnp.bfloat16)

    @pl.when(s == 0)
    def _():
        o32[...] = up_ref[...].astype(jnp.float32)
        for t in range(frames):
            g_own[1, t] = o32[pl.ds(t, GROUP, stride=frames), :].astype(jnp.bfloat16)

    for q in range(chans):
        wt[q, :, DEPTH:] = jnp.zeros((GROUP, PADDED - DEPTH), jnp.bfloat16)
    step = 2 * GROUP
    for k in range(0, DEPTH, step):
        size = min(step, DEPTH - k)
        turned = w_ref[k : k + size, :].astype(jnp.float32).T.astype(jnp.bfloat16)
        for q in range(chans):
            wt[q, :, k : k + size] = turned[q * GROUP : (q + 1) * GROUP]

    pl.semaphore_wait(barrier, len(peers))

    def frames_of(b):
        return (blocks - 1 - b) * BLOCK

    def weight_copy(q):
        return remote(wt.at[2 * q + 1 - core], wp.at[q], w_send.at[q], w_recv.at[q], (s, f, partner))

    def row_copy(src, b, slot, section, row, out_sem=g_send):
        first = frames_of(b)
        return remote(
            src,
            g_own.at[slot, pl.ds(first, BLOCK)],
            out_sem.at[b, slot],
            g_recv.at[b, slot],
            (section, row, d),
        )

    def spread(src, b, section, centre, go):
        out_sem = g_send if centre else u_send
        if centre:
            go(row_copy(src, b, 1, section, f, out_sem))

        @pl.when(has_down)
        def _():
            go(row_copy(src, b, 2, section, (f + 1) % rows, out_sem))

        @pl.when(has_up)
        def _():
            go(row_copy(src, b, 0, section, (f + rows - 1) % rows, out_sem))

    def begin(copy):
        copy.start()

    def sent(copy):
        copy.wait_send()

    def arrived(copy):
        copy.wait_recv()

    def block_of(g, b):
        return g.at[1, pl.ds(frames_of(b), BLOCK)]

    for q in range(chips):
        weight_copy(q).start()

    @pl.when(s == 0)
    def _():
        for b in range(blocks):
            spread(block_of(g_own, b), b, s, False, begin)

    def forward_copy(b, slot):
        first = pl.ds(frames_of(b), BLOCK)
        return remote(
            g_own.at[slot, first], g_par.at[slot, first], f_send.at[b, slot], f_recv.at[b, slot], (s, f, partner)
        )

    def per_slot(fn):
        fn(1)
        pl.when(has_down)(lambda: fn(0))
        pl.when(has_up)(lambda: fn(2))

    def take(b):
        def one(slot):
            copy = row_copy(block_of(g_own, b), b, slot, s, f)
            if slot == 1:
                pl.when(s > 0)(lambda: copy.wait_recv())
            else:
                copy.wait_recv()
            forward_copy(b, slot).start()

        per_slot(one)

    lane = lax.broadcasted_iota(jnp.int32, (GROUP, width), 1)

    def build(g, x, t):
        for slot in range(3):
            row = g[slot, t].astype(jnp.float32)
            after = jnp.where(lane == width - 1, 0.0, pltpu.roll(row, width - 1, 1))
            before = jnp.where(lane == 0, 0.0, pltpu.roll(row, 1, 1))
            base = t * SLAB + slot * 3 * GROUP
            x[base : base + GROUP] = after.astype(jnp.bfloat16)
            x[base + GROUP : base + 2 * GROUP] = row.astype(jnp.bfloat16)
            x[base + 2 * GROUP : base + 3 * GROUP] = before.astype(jnp.bfloat16)

    def columns(x, b):
        first = frames_of(b)
        return jnp.concatenate(
            [x[t * SLAB : t * SLAB + PADDED] for t in range(first, first + BLOCK)], axis=1
        )

    def term_copy(b, q):
        return remote(
            part.at[b, q], recv.at[b, chip], r_send.at[b, q], r_recv.at[b, chip], (s, f, 2 * q + core)
        )

    def term_arrival(b, q):
        return remote(
            part.at[b, q], recv.at[b, q], r_send.at[b, q], r_recv.at[b, q], (s, f, 2 * q + core)
        )

    ways = (1, -1)
    splits = (pl.ds(0, 5), pl.ds(5, 4))

    def along(way):
        return (s, h * ring + (z + way + ring) % ring, d)

    def place(offset):
        return (z + offset + 2 * ring) % ring

    def piece(ref, first, count, half, owner):
        columns = pl.ds(pl.multiple_of((owner % lanes) * width, width), width)
        return ref.at[pl.ds(first, count), half, owner // lanes, :, columns]

    def chain_copy(p, e, k):
        if k == 0:
            src = piece(wsum, 9 * p, 9, e, place(ways[e] * reach))
            dst = chain.at[p, e, 0, e]
        else:
            src, dst = chain.at[p, e, k - 1], chain.at[p, e, k]
        return remote(src, dst, c_send.at[p, e, k], c_recv.at[p, e, k], along(ways[e]))

    def own_term(p, half, offset):
        return piece(wsum, 9 * p, 9, half, place(offset))[...].astype(jnp.float32)

    def chain_step(p, k):
        for e, way in enumerate(ways):
            chain_copy(p, e, k - 1).wait_recv()
            for half in range(2):
                term = own_term(p, half, way * (reach - k))
                if k > 1 or half == e:
                    term = term + chain[p, e, k - 1, half].astype(jnp.float32)
                chain[p, e, k - 1, half] = term.astype(jnp.bfloat16)
            chain_copy(p, e, k).start()

    def half_copy(p):
        return remote(half_sum.at[p, 1 - h], half_in.at[p], y_send.at[p], y_recv.at[p], across)

    def chain_end(p):
        for e in range(2):
            chain_copy(p, e, reach - 1).wait_recv()
        for half in range(2):
            term = own_term(p, half, 0)
            for e in range(2):
                term = term + chain[p, e, reach - 1, half].astype(jnp.float32)
            half_sum[p, half] = term.astype(jnp.bfloat16)
        half_copy(p).start()

    def share_copy(p, half):
        at = piece(wfin, 9 * p, 9, half, z)
        return remote(at, at, b_send.at[p], b_recv.at[p], across)

    def gather_copy(p, e, k, half, arrival=False):
        at = piece(wfin, 9 * p, 9, half, place(-ways[e] * (k + 1 if arrival else k)))
        return remote(at, at, a_send.at[p, e, k, half], a_recv.at[p, e, k, half], along(ways[e]))

    def half_end(p):
        half_copy(p).wait_recv()
        final = half_sum[p, h].astype(jnp.float32) + half_in[p].astype(jnp.float32)
        piece(wfin, 9 * p, 9, h, z)[...] = final.astype(jnp.bfloat16)
        share_copy(p, h).start()
        for e in range(2):
            gather_copy(p, e, 0, h).start()

    def share_end(p):
        share_copy(p, 1 - h).wait_recv()
        for e in range(2):
            gather_copy(p, e, 0, 1 - h).start()

    def gather_step(p, k):
        for half in (h, 1 - h):
            for e in range(2):
                gather_copy(p, e, k - 1, half, True).wait_recv()
                if k < reach - 1:
                    gather_copy(p, e, k, half).start()
        if k == reach - 1:
            for e in range(2):
                gather_copy(p, e, k, e).start()

    def gather_end(p):
        for e in range(2):
            gather_copy(p, e, reach - 1, e, True).wait_recv()

    def whole_copy():
        return remote(wsum.at[pl.ds(0, 9), 1 - h], whole_in, y_send.at[0], y_recv.at[0], across)

    def short_copy(e, k):
        if k == 0:
            taps = splits[e]
            src = piece(wsum, taps.start, taps.size, h, place(ways[e] * reach))
            dst = short_chain.at[e, 0, taps]
        else:
            src, dst = short_chain.at[e, k - 1], short_chain.at[e, k]
        return remote(src, dst, c_send.at[0, e, k], c_recv.at[0, e, k], along(ways[e]))

    def whole_end():
        whole_copy().wait_recv()
        for n in range(9):
            both = wsum[n, h].astype(jnp.float32) + whole_in[n].astype(jnp.float32)
            wsum[n, h] = both.astype(jnp.bfloat16)
        for e in range(2):
            short_copy(e, 0).start()

    def short_step(k):
        for e, way in enumerate(ways):
            short_copy(e, k - 1).wait_recv()
            for n in range(9):
                term = piece(wsum, n, 1, h, place(way * (reach - k)))[...].astype(jnp.float32)
                low = splits[e].start
                if k > 1 or low <= n < low + splits[e].size:
                    term = term + short_chain[e, k - 1, n].astype(jnp.float32)
                short_chain[e, k - 1, n] = term[0].astype(jnp.bfloat16)
            short_copy(e, k).start()

    def cross_copy(n, owner, half):
        at = piece(wfin, 0, 9, half, owner)
        return remote(at, at, e_send.at[n], e_recv.at[n], across)

    def spread_copy(e, k, arrival=False):
        owner = place(-ways[e] * (k + 1 if arrival else k))
        first, count = (splits[e].start, splits[e].size) if k == reach - 1 else (0, 9)
        at = piece(wfin, first, count, h, owner)
        return remote(at, at, a_send.at[0, e, k, 0], a_recv.at[0, e, k, 0], along(ways[e]))

    def short_end():
        final = own_term(0, h, 0)
        for e in range(2):
            short_copy(e, reach - 1).wait_recv()
            final = final + short_chain[e, reach - 1].astype(jnp.float32)
        piece(wfin, 0, 9, h, z)[...] = final.astype(jnp.bfloat16)
        for e in range(2):
            spread_copy(e, 0).start()
        cross_copy(0, z, h).start()

    def spread_step(k):
        for e in range(2):
            spread_copy(e, k - 1, True).wait_recv()
            spread_copy(e, k).start()
            cross_copy(1 + 2 * (k - 1) + e, place(-ways[e] * k), h).start()

    def spread_end():
        for e in range(2):
            spread_copy(e, reach - 1, True).wait_recv()
        cross_copy(ring - 1, place(reach), h).start()

    def cross_all(half, go):
        go(cross_copy(0, z, half))
        for k in range(1, reach):
            for e in range(2):
                go(cross_copy(1 + 2 * (k - 1) + e, place(-ways[e] * k), half))
        go(cross_copy(ring - 1, place(reach), half))

    later = (2, 1)

    def sum_begin():
        whole_copy().start()
        for p in later:
            for e in range(2):
                chain_copy(p, e, 0).start()

    def sum_finish():
        for k in range(1, reach):
            for p in later:
                chain_step(p, k)
            if k == max(1, reach - 2):
                whole_end()
        short_step(1)
        for p in later:
            chain_end(p)
        for k in range(2, reach):
            short_step(k)
        for p in later:
            half_end(p)
        short_end()
        for p in later:
            share_end(p)
        for k in range(1, reach):
            spread_step(k)
            for p in later:
                gather_step(p, k)
        spread_end()
        for p in later:
            gather_end(p)
        cross_all(1 - h, arrived)

    def sum_sent():
        whole_copy().wait_send()
        for e in range(2):
            for k in range(reach):
                short_copy(e, k).wait_send()
                spread_copy(e, k).wait_send()
        cross_all(h, sent)
        for p in later:
            half_copy(p).wait_send()
            share_copy(p, h).wait_send()
            for e in range(2):
                for k in range(reach):
                    chain_copy(p, e, k).wait_send()
                    for half in range(2) if k < reach - 1 else (e,):
                        gather_copy(p, e, k, half).wait_send()

    hops = sorted(range(1, chips), key=lambda o: -min(o, chips - o))

    for b in range(blocks):
        first = frames_of(b)
        take(b)
        for t in range(first, first + BLOCK):
            build(g_own, x_own, t)
        lhs = jnp.concatenate([wt[2 * q + core] for q in range(chips)], axis=0)
        total = jnp.dot(lhs, columns(x_own, b), preferred_element_type=jnp.float32)
        if b == 0:
            for q in range(chips):
                weight_copy(q).wait_recv()
        per_slot(lambda slot: forward_copy(b, slot).wait_recv())
        for t in range(first, first + BLOCK):
            build(g_par, x_par, t)
        lhs = jnp.concatenate([wp[q] for q in range(chips)], axis=0)
        total = total + jnp.dot(lhs, columns(x_par, b), preferred_element_type=jnp.float32)
        for q in range(chips):
            part[b, q] = total[q * GROUP : (q + 1) * GROUP].astype(jnp.bfloat16)
        for o in hops:
            term_copy(b, (chip + o) % chips).start()

        if b == 0:
            a32[...] = acts_ref[...].astype(jnp.float32)
            for t in range(frames):
                own = a32[pl.ds(d * (GROUP * frames) + t, GROUP, stride=frames), :]
                logistic = 1.0 / (1.0 + jnp.exp(-own))
                slope[t] = logistic * (1.0 + own * (1.0 - logistic))
                for q in range(0, channels, step):
                    values = a32[pl.ds(q * frames + t, step, stride=frames), :]
                    values = values / (1.0 + jnp.exp(-values))
                    feat[t * width : (t + 1) * width, q : q + step] = values.T.astype(jnp.bfloat16)

        cells = slice(first * width, (first + BLOCK) * width)
        for k in range(3):
            lhs = jnp.concatenate(
                [x_own[(t + k) * SLAB : (t + k + 1) * SLAB] for t in range(first, first + BLOCK)], axis=1
            )
            add = jnp.dot(lhs, feat[cells, :], preferred_element_type=jnp.float32)
            at = slice(k * SLAB, (k + 1) * SLAB)
            if b > 0:
                add = add + acc[at]
            if b == blocks - 1:
                wsum[9 * k : 9 * k + 9] = add.astype(jnp.bfloat16).reshape(9, 2, 2, 16, channels)
            else:
                acc[at] = add

        if b == blocks - 1:
            sum_begin()

        back = part[b, chip].astype(jnp.float32)
        for o in reversed(hops):
            q = (chip + o) % chips
            term_arrival(b, q).wait_recv()
            back = back + recv[b, q].astype(jnp.float32)
        for n, t in enumerate(range(first, first + BLOCK)):
            new = g_own[1, t].astype(jnp.float32) + slope[t] * back[:, n * width : (n + 1) * width]
            new = new.astype(jnp.bfloat16)
            gout[t] = new
            o32[pl.ds(t, GROUP, stride=frames), :] = new.astype(jnp.float32)

        @pl.when(s < sections - 1)
        def _():
            spread(gout.at[pl.ds(first, BLOCK)], b, (s + 1) % sections, True, begin)

    grads_ref[...] = o32[...].astype(jnp.bfloat16)
    sum_finish()
    wg_ref[...] = wfin[...]
    sum_sent()

    for q in range(chips):
        weight_copy(q).wait_send()

    @pl.when(s == 0)
    def _():
        for b in range(blocks):
            spread(block_of(g_own, b), b, s, False, sent)

    for b in range(blocks):
        per_slot(lambda slot: forward_copy(b, slot).wait_send())
        for o in hops:
            term_copy(b, (chip + o) % chips).wait_send()

    pl.when(s < sections - 1)(
        lambda: [
            spread(gout.at[pl.ds(frames_of(b), BLOCK)], b, (s + 1) % sections, True, sent) for b in range(blocks)
        ] and None
    )


def pipeline(sections, rows, chips, frames, upstream, acts, weights):
    channels = weights.shape[1]
    width = 128
    blocks = frames // BLOCK
    bf16, f32 = jnp.bfloat16, jnp.float32
    dma = pltpu.SemaphoreType.DMA
    vmem = pl.BlockSpec(memory_space=pltpu.VMEM)
    depth = (frames + 2) * SLAB + GROUP
    reach = rows // 4
    return pl.pallas_call(
        functools.partial(pipeline_kernel, sections, rows, chips, frames),
        out_shape=(
            jax.ShapeDtypeStruct((GROUP * frames, width), bf16),
            jax.ShapeDtypeStruct((27, 2, 2, 16, channels), bf16),
        ),
        in_specs=[vmem] * 3,
        out_specs=(vmem, vmem),
        scratch_shapes=[
            pltpu.VMEM((3, frames + 2, GROUP, width), bf16),
            pltpu.VMEM((3, frames + 2, GROUP, width), bf16),
            pltpu.VMEM((depth, width), bf16),
            pltpu.VMEM((depth, width), bf16),
            pltpu.VMEM((2 * chips, GROUP, PADDED), bf16),
            pltpu.VMEM((chips, GROUP, PADDED), bf16),
            pltpu.VMEM((blocks, chips, GROUP, BLOCK * width), bf16),
            pltpu.VMEM((blocks, chips, GROUP, BLOCK * width), bf16),
            pltpu.VMEM((channels * frames, width), f32),
            pltpu.VMEM((frames, GROUP, width), f32),
            pltpu.VMEM((frames * width, channels), bf16),
            pltpu.VMEM((DEPTH, channels), f32),
            pltpu.VMEM((GROUP * frames, width), f32),
            pltpu.VMEM((frames, GROUP, width), bf16),
            pltpu.VMEM((27, 2, 2, 16, channels), bf16),
            pltpu.VMEM((27, 2, 2, 16, channels), bf16),
            pltpu.VMEM((3, 2, reach, 2, 9, 16, width), bf16),
            pltpu.VMEM((2, reach, 9, 16, width), bf16),
            pltpu.VMEM((3, 2, 9, 16, width), bf16),
            pltpu.VMEM((3, 9, 16, width), bf16),
            pltpu.VMEM((9, 2, 16, channels), bf16),
            dma((blocks, 3)),
            dma((blocks, 3)),
            dma((blocks, 3)),
            dma((blocks, 3)),
            dma((blocks, 3)),
            dma((blocks, chips)),
            dma((blocks, chips)),
            dma((chips,)),
            dma((chips,)),
            dma((3, 2, reach)),
            dma((3, 2, reach)),
            dma((3,)),
            dma((3,)),
            dma((3, 2, reach, 2)),
            dma((3, 2, reach, 2)),
            dma((3,)),
            dma((3,)),
            dma((rows // 2,)),
            dma((rows // 2,)),
        ],
        compiler_params=pltpu.CompilerParams(collective_id=0, has_side_effects=True),
        name="pipeline",
    )(upstream, acts, weights)


def solution(mesh):
    sections, rows, chans = (mesh.shape[a] for a in ("section", "frame", "chan"))

    def body(upstream, acts, weights):
        group, frames, _, width = upstream.shape
        channels = acts.shape[1]
        grads, kernel_sum = pipeline(
            sections,
            rows,
            chans // 2,
            frames,
            upstream.reshape(group * frames, width),
            acts.reshape(channels * frames, width),
            weights.reshape(27 * group, channels),
        )
        return grads.reshape(1, group, frames, 1, width), kernel_sum.reshape(1, 27, group, channels)

    return jax.shard_map(
        body,
        mesh=mesh,
        in_specs=(
            P("chan", None, "frame", None),
            P("section", None, None, "frame", None),
            P("section", None, "chan", None),
        ),
        out_specs=(P("section", "chan", None, "frame", None), P("section", None, "chan", None)),
        check_vma=False,
    )
```

```python
import functools

import jax
import jax.numpy as jnp
from jax import lax
from jax.experimental import pallas as pl
from jax.experimental.pallas import tpu as pltpu
from jax.sharding import PartitionSpec as P

MESH = pl.DeviceIdType.MESH
CUTS = (2, 2, 2, 2)
AHEAD = 2
CROSS = 2
GROUP = 64
SLAB = 9 * GROUP
DEPTH = 27 * GROUP
PADDED = 28 * GROUP


def remote(src, dst, send_sem, recv_sem, device):
    return pltpu.make_async_remote_copy(
        src_ref=src, dst_ref=dst, send_sem=send_sem, recv_sem=recv_sem, device_id=device, device_id_type=MESH
    )


def pipeline_kernel(
    sections, rows, chips, frames,
    up_ref, acts_ref, w_ref, grads_ref, wg_ref,
    g_own, g_par, x_own, x_par, wt, wp, part, recv, a32, slope, feat, acc, o32, gout,
    wsum, wfin, chain, short_chain, last_in, half_in, whole_in, g16,
    u_send, g_send, g_recv, f_send, f_recv, r_send, r_recv, w_send, w_recv,
    c_send, c_recv, y_send, y_recv, a_send, a_recv, b_send, b_recv, e_send, e_recv, l_send, l_recv, o_sem,
):
    channels = w_ref.shape[1]
    chans = 2 * chips
    blocks = len(CUTS)
    width = 128
    s = lax.axis_index("section")
    f = lax.axis_index("frame")
    d = lax.axis_index("chan")
    chip = d // 2
    core = d % 2
    partner = d + 1 - 2 * core

    barrier = pltpu.get_barrier_semaphore()
    peers = []
    for ds in (1, sections - 1):
        for df in (0, 1, rows - 1):
            peers.append(((s + ds) % sections, (f + df) % rows, d))
    for df in (1, rows - 1):
        peers.append((s, (f + df) % rows, d))
    peers.append((s, f, partner))
    for dq in range(1, chips):
        peers.append((s, f, ((chip + dq) % chips) * 2 + core))
    ring = rows // 2
    lanes = ring // 2
    reach = ring // 2
    h = f // ring
    z = f % ring
    across = (s, (1 - h) * ring + z, d)
    peers.append(across)
    for dz in (1, ring - 1):
        for row in (h, 1 - h):
            peers.append((s, row * ring + (z + dz) % ring, d))
    for peer in peers:
        pl.semaphore_signal(barrier, inc=1, device_id=peer, device_id_type=MESH)

    has_up = f > 0
    has_down = f < rows - 1

    for g in (g_own, g_par):
        for row in range(3):
            g[row, frames:] = jnp.zeros((2, GROUP, width), jnp.bfloat16)

        @pl.when(jnp.logical_not(has_down))
        def _():
            g[0, :frames] = jnp.zeros((frames, GROUP, width), jnp.bfloat16)

        @pl.when(jnp.logical_not(has_up))
        def _():
            g[2, :frames] = jnp.zeros((frames, GROUP, width), jnp.bfloat16)

    for x in (x_own, x_par):
        x[frames * SLAB :] = jnp.zeros((x.shape[0] - frames * SLAB, width), jnp.bfloat16)

    @pl.when(s == 0)
    def _():
        o32[...] = up_ref[...].astype(jnp.float32)
        for t in range(frames):
            g_own[1, t] = o32[pl.ds(t, GROUP, stride=frames), :].astype(jnp.bfloat16)

    for q in range(chans):
        wt[q, :, DEPTH:] = jnp.zeros((GROUP, PADDED - DEPTH), jnp.bfloat16)
    step = 2 * GROUP
    for k in range(0, DEPTH, step):
        size = min(step, DEPTH - k)
        turned = w_ref[k : k + size, :].astype(jnp.float32).T.astype(jnp.bfloat16)
        for q in range(chans):
            wt[q, :, k : k + size] = turned[q * GROUP : (q + 1) * GROUP]

    pl.semaphore_wait(barrier, len(peers))

    def frames_of(b):
        return frames - sum(CUTS[: b + 1])

    def range_of(b):
        return range(frames_of(b), frames_of(b) + CUTS[b])

    def weight_copy(q):
        return remote(wt.at[2 * q + 1 - core], wp.at[q], w_send.at[q], w_recv.at[q], (s, f, partner))

    def row_copy(src, b, slot, section, row, out_sem=g_send):
        first = frames_of(b)
        return remote(
            src,
            g_own.at[slot, pl.ds(first, CUTS[b])],
            out_sem.at[b, slot],
            g_recv.at[b, slot],
            (section, row, d),
        )

    def spread(src, b, section, centre, go):
        out_sem = g_send if centre else u_send
        if centre:
            go(row_copy(src, b, 1, section, f, out_sem))

        @pl.when(has_down)
        def _():
            go(row_copy(src, b, 2, section, (f + 1) % rows, out_sem))

        @pl.when(has_up)
        def _():
            go(row_copy(src, b, 0, section, (f + rows - 1) % rows, out_sem))

    def begin(copy):
        copy.start()

    def sent(copy):
        copy.wait_send()

    def arrived(copy):
        copy.wait_recv()

    def block_of(g, b):
        return g.at[1, pl.ds(frames_of(b), CUTS[b])]

    for q in range(chips):
        weight_copy(q).start()

    @pl.when(s == 0)
    def _():
        for b in range(blocks):
            spread(block_of(g_own, b), b, s, False, begin)

    def forward_copy(b, slot):
        first = pl.ds(frames_of(b), CUTS[b])
        return remote(
            g_own.at[slot, first], g_par.at[slot, first], f_send.at[b, slot], f_recv.at[b, slot], (s, f, partner)
        )

    def per_slot(fn):
        fn(1)
        pl.when(has_down)(lambda: fn(0))
        pl.when(has_up)(lambda: fn(2))

    def take(b):
        def one(slot):
            copy = row_copy(block_of(g_own, b), b, slot, s, f)
            if slot == 1:
                pl.when(s > 0)(lambda: copy.wait_recv())
            else:
                copy.wait_recv()
            forward_copy(b, slot).start()

        per_slot(one)

    lane = lax.broadcasted_iota(jnp.int32, (GROUP, width), 1)

    def build(g, x, t):
        for slot in range(3):
            row = g[slot, t].astype(jnp.float32)
            after = jnp.where(lane == width - 1, 0.0, pltpu.roll(row, width - 1, 1))
            before = jnp.where(lane == 0, 0.0, pltpu.roll(row, 1, 1))
            base = t * SLAB + slot * 3 * GROUP
            x[base : base + GROUP] = after.astype(jnp.bfloat16)
            x[base + GROUP : base + 2 * GROUP] = row.astype(jnp.bfloat16)
            x[base + 2 * GROUP : base + 3 * GROUP] = before.astype(jnp.bfloat16)

    def columns(x, b):
        return jnp.concatenate([x[t * SLAB : t * SLAB + PADDED] for t in range_of(b)], axis=1)

    def term_copy(b, q):
        at = pl.ds(frames_of(b), CUTS[b])
        return remote(
            part.at[at, q], recv.at[at, chip], r_send.at[b, q], r_recv.at[b, chip], (s, f, 2 * q + core)
        )

    def term_arrival(b, q):
        at = pl.ds(frames_of(b), CUTS[b])
        return remote(part.at[at, q], recv.at[at, q], r_send.at[b, q], r_recv.at[b, q], (s, f, 2 * q + core))

    ways = (1, -1)
    splits = (pl.ds(0, 5), pl.ds(5, 4))

    def along(way, side=0):
        row = 1 - h if side else h
        return (s, row * ring + (z + way + ring) % ring, d)

    def place(offset):
        return (z + offset + 2 * ring) % ring

    def piece(ref, first, count, half, owner):
        columns = pl.ds(pl.multiple_of((owner % lanes) * width, width), width)
        return ref.at[pl.ds(first, count), half, owner // lanes, :, columns]

    def chain_copy(p, e, k):
        if k == 0:
            src = piece(wsum, 9 * p, 9, e, place(ways[e] * reach))
            dst = chain.at[p, e, 0, e]
        else:
            src, dst = chain.at[p, e, k - 1], chain.at[p, e, k]
        return remote(src, dst, c_send.at[p, e, k], c_recv.at[p, e, k], along(ways[e]))

    def own_term(p, half, offset):
        return piece(wsum, 9 * p, 9, half, place(offset))[...].astype(jnp.float32)

    def chain_step(p, k):
        for e, way in enumerate(ways):
            chain_copy(p, e, k - 1).wait_recv()
            for half in range(2):
                term = own_term(p, half, way * (reach - k))
                if k > 1 or half == e:
                    term = term + chain[p, e, k - 1, half].astype(jnp.float32)
                chain[p, e, k - 1, half] = term.astype(jnp.bfloat16)
            if k < reach - 1:
                chain_copy(p, e, k).start()
            else:
                for side in range(2):
                    last_copy(p, e, side).start()

    def last_copy(p, e, side):
        half = 1 - h if side else h
        return remote(
            chain.at[p, e, reach - 2, half],
            last_in.at[p, e, side],
            l_send.at[p, e, side],
            l_recv.at[p, e, side],
            along(ways[e], side),
        )

    def half_copy(p):
        return remote(
            piece(wsum, 9 * p, 9, 1 - h, z), half_in.at[p], y_send.at[p], y_recv.at[p], across
        )

    def chain_end(p):
        half_copy(p).wait_recv()
        total = own_term(p, h, 0) + half_in[p].astype(jnp.float32)
        for side in range(2):
            for e in range(2):
                last_copy(p, e, side).wait_recv()
                total = total + last_in[p, e, side].astype(jnp.float32)
        piece(wfin, 9 * p, 9, h, z)[...] = total.astype(jnp.bfloat16)
        for side in range(2):
            for e in range(2):
                first_copy(p, e, side).start()
        share_copy(p, h).start()

    def first_copy(p, e, side):
        at = piece(wfin, 9 * p, 9, h, z)
        slot = 1 - h if side else h
        return remote(at, at, a_send.at[p, e, 0, slot], a_recv.at[p, e, 0, h], along(ways[e], side))

    def share_copy(p, half):
        at = piece(wfin, 9 * p, 9, half, z)
        return remote(at, at, b_send.at[p], b_recv.at[p], across)

    def gather_copy(p, e, k, half, arrival=False):
        at = piece(wfin, 9 * p, 9, half, place(-ways[e] * (k + 1 if arrival else k)))
        return remote(at, at, a_send.at[p, e, k, half], a_recv.at[p, e, k, half], along(ways[e]))

    def gather_step(p, k):
        for half in (h, 1 - h):
            for e in range(2):
                gather_copy(p, e, k - 1, half, True).wait_recv()
                if k < reach - 1:
                    gather_copy(p, e, k, half).start()
        if k == reach - 1:
            for e in range(2):
                gather_copy(p, e, k, e).start()

    def gather_end(p):
        share_copy(p, 1 - h).wait_recv()
        for e in range(2):
            gather_copy(p, e, reach - 1, e, True).wait_recv()

    def whole_copy():
        return remote(wsum.at[pl.ds(9 * CROSS, 9), 1 - h], whole_in, y_send.at[CROSS], y_recv.at[CROSS], across)

    def short_copy(e, k):
        if k == 0:
            taps = splits[e]
            src = piece(wsum, 9 * CROSS + taps.start, taps.size, h, place(ways[e] * reach))
            dst = short_chain.at[e, 0, taps]
        else:
            src, dst = short_chain.at[e, k - 1], short_chain.at[e, k]
        return remote(src, dst, c_send.at[CROSS, e, k], c_recv.at[CROSS, e, k], along(ways[e]))

    def whole_end():
        whole_copy().wait_recv()
        for n in range(9):
            both = wsum[9 * CROSS + n, h].astype(jnp.float32) + whole_in[n].astype(jnp.float32)
            wsum[9 * CROSS + n, h] = both.astype(jnp.bfloat16)
        for e in range(2):
            short_copy(e, 0).start()

    def short_step(k):
        for e, way in enumerate(ways):
            short_copy(e, k - 1).wait_recv()
            for n in range(9):
                term = piece(wsum, 9 * CROSS + n, 1, h, place(way * (reach - k)))[...].astype(jnp.float32)
                low = splits[e].start
                if k > 1 or low <= n < low + splits[e].size:
                    term = term + short_chain[e, k - 1, n].astype(jnp.float32)
                short_chain[e, k - 1, n] = term[0].astype(jnp.bfloat16)
            short_copy(e, k).start()

    def cross_copy(n, owner, half):
        at = piece(wfin, 9 * CROSS, 9, half, owner)
        return remote(at, at, e_send.at[n], e_recv.at[n], across)

    def spread_copy(e, k, arrival=False):
        owner = place(-ways[e] * (k + 1 if arrival else k))
        first, count = (splits[e].start, splits[e].size) if k == reach - 1 else (0, 9)
        at = piece(wfin, 9 * CROSS + first, count, h, owner)
        return remote(at, at, a_send.at[CROSS, e, k, 0], a_recv.at[CROSS, e, k, 0], along(ways[e]))

    def short_end():
        final = own_term(CROSS, h, 0)
        for e in range(2):
            short_copy(e, reach - 1).wait_recv()
            final = final + short_chain[e, reach - 1].astype(jnp.float32)
        piece(wfin, 9 * CROSS, 9, h, z)[...] = final.astype(jnp.bfloat16)
        for e in range(2):
            spread_copy(e, 0).start()
        cross_copy(0, z, h).start()

    def spread_step(k):
        for e in range(2):
            spread_copy(e, k - 1, True).wait_recv()
            spread_copy(e, k).start()
            cross_copy(1 + 2 * (k - 1) + e, place(-ways[e] * k), h).start()

    def spread_end():
        for e in range(2):
            spread_copy(e, reach - 1, True).wait_recv()
        cross_copy(ring - 1, place(reach), h).start()

    def cross_all(half, go):
        go(cross_copy(0, z, half))
        for k in range(1, reach):
            for e in range(2):
                go(cross_copy(1 + 2 * (k - 1) + e, place(-ways[e] * k), half))
        go(cross_copy(ring - 1, place(reach), half))

    later = tuple(p for p in (2, 1, 0) if p != CROSS)

    def sum_begin(p):
        if p == CROSS:
            whole_copy().start()
        else:
            for e in range(2):
                chain_copy(p, e, 0).start()
            half_copy(p).start()

    def sum_finish(between):
        one, two = later
        for k in range(1, reach):
            chain_step(one, k)
            if k == 1:
                between(0)
            if k > 1:
                short_step(k - 1)
            chain_step(two, k)
            if k == 1:
                whole_end()
            between(k)
        chain_end(one)
        short_step(reach - 1)
        chain_end(two)
        short_end()
        for k in range(1, reach):
            gather_step(one, k)
            spread_step(k)
            gather_step(two, k)
        gather_end(one)
        out_copy(one).start()
        spread_end()
        gather_end(two)
        out_copy(two).start()
        cross_all(1 - h, arrived)
        out_copy(CROSS).start()

    def out_copy(p):
        taps = pl.ds(9 * p, 9)
        return pltpu.make_async_copy(wfin.at[taps], wg_ref.at[taps], o_sem.at[p])

    def grads_copy():
        return pltpu.make_async_copy(g16, grads_ref, o_sem.at[3])

    def grads_out():
        g16[...] = o32[...].astype(jnp.bfloat16)
        grads_copy().start()

    def sum_sent():
        whole_copy().wait_send()
        for e in range(2):
            for k in range(reach):
                short_copy(e, k).wait_send()
                spread_copy(e, k).wait_send()
        cross_all(h, sent)
        for p in later:
            half_copy(p).wait_send()
            share_copy(p, h).wait_send()
            for e in range(2):
                for side in range(2):
                    last_copy(p, e, side).wait_send()
                    first_copy(p, e, side).wait_send()
                for k in range(reach - 1):
                    chain_copy(p, e, k).wait_send()
                for k in range(1, reach):
                    for half in range(2) if k < reach - 1 else (e,):
                        gather_copy(p, e, k, half).wait_send()

    hops = sorted(range(1, chips), key=lambda o: -min(o, chips - o))

    last = sections - 1
    final = blocks - 1

    def prepare():
        a32[...] = acts_ref[...].astype(jnp.float32)
        for t in range(frames):
            own = a32[pl.ds(d * (GROUP * frames) + t, GROUP, stride=frames), :]
            logistic = 1.0 / (1.0 + jnp.exp(-own))
            slope[t] = logistic * (1.0 + own * (1.0 - logistic))
            for q in range(0, channels, step):
                values = a32[pl.ds(q * frames + t, step, stride=frames), :]
                values = values / (1.0 + jnp.exp(-values))
                feat[t * width : (t + 1) * width, q : q + step] = values.T.astype(jnp.bfloat16)

    def back_terms(b):
        lhs = jnp.concatenate([wt[2 * q + core] for q in range(chips)], axis=0)
        total = jnp.dot(lhs, columns(x_own, b), preferred_element_type=jnp.float32)
        if b == 0:
            for q in range(chips):
                weight_copy(q).wait_recv()
        per_slot(lambda slot: forward_copy(b, slot).wait_recv())
        for t in range_of(b):
            build(g_par, x_par, t)
        lhs = jnp.concatenate([wp[q] for q in range(chips)], axis=0)
        total = total + jnp.dot(lhs, columns(x_par, b), preferred_element_type=jnp.float32)
        for n, t in enumerate(range_of(b)):
            for q in range(chips):
                block = total[q * GROUP : (q + 1) * GROUP, n * width : (n + 1) * width]
                part[t, q] = block.astype(jnp.bfloat16)
        for o in hops:
            term_copy(b, (chip + o) % chips).start()

    def kernel_terms(b):
        for k in range(3):
            at = slice(k * SLAB, (k + 1) * SLAB)
            source = [t for t in range_of(b) if t >= k]
            add = None
            if source:
                lhs = jnp.concatenate([x_own[t * SLAB : (t + 1) * SLAB] for t in source], axis=1)
                cells = slice((source[0] - k) * width, (source[-1] - k + 1) * width)
                add = jnp.dot(lhs, feat[cells, :], preferred_element_type=jnp.float32)
                if b > 0:
                    add = add + acc[at]
            if source and source[0] == k:
                wsum[9 * k : 9 * k + 9] = add.astype(jnp.bfloat16).reshape(9, 2, 2, 16, channels)
            elif source:
                acc[at] = add

    def update(b):
        for o in reversed(hops):
            term_arrival(b, (chip + o) % chips).wait_recv()
        for t in range_of(b):
            back = part[t, chip].astype(jnp.float32)
            for o in hops:
                back = back + recv[t, (chip + o) % chips].astype(jnp.float32)
            new = (g_own[1, t].astype(jnp.float32) + slope[t] * back).astype(jnp.bfloat16)
            gout[t] = new
            o32[pl.ds(t, GROUP, stride=frames), :] = new.astype(jnp.float32)
        part_out = gout.at[pl.ds(frames_of(b), CUTS[b])]
        pl.when(s < last)(lambda: spread(part_out, b, (s + 1) % sections, True, begin))

    def complete(b):
        return [k for k in (2, 1, 0) if k in range_of(b)]

    pl.when(s > 0)(prepare)
    for b in range(blocks):
        take(b)
        for t in range_of(b):
            build(g_own, x_own, t)

        @pl.when(s == last)
        def _():
            kernel_terms(b)
            for k in complete(b):
                sum_begin(k)

        if b < final:
            back_terms(b)
        else:
            pl.when(s < last)(lambda: back_terms(final))
        if b == 0:
            pl.when(s == 0)(prepare)
        if b >= AHEAD - 1:
            if b < final:
                update(b - AHEAD + 1)
            else:
                pl.when(s < last)(lambda: update(final - AHEAD + 1))

    @pl.when(s < last)
    def _():
        for b in range(blocks - AHEAD + 1, blocks):
            update(b)
        grads_out()
        for b in range(blocks):
            kernel_terms(b)
            for k in complete(b):
                sum_begin(k)

    def between(k):
        @pl.when(s == last)
        def _():
            if k == 0:
                back_terms(final)
            if k == min(2, reach - 1):
                for b in range(final - AHEAD + 1, blocks):
                    update(b)
                grads_out()

    sum_finish(between)
    sum_sent()
    for p in range(3):
        out_copy(p).wait()
    grads_copy().wait()

    for q in range(chips):
        weight_copy(q).wait_send()

    @pl.when(s == 0)
    def _():
        for b in range(blocks):
            spread(block_of(g_own, b), b, s, False, sent)

    for b in range(blocks):
        per_slot(lambda slot: forward_copy(b, slot).wait_send())
        for o in hops:
            term_copy(b, (chip + o) % chips).wait_send()

    pl.when(s < sections - 1)(
        lambda: [
            spread(gout.at[pl.ds(frames_of(b), CUTS[b])], b, (s + 1) % sections, True, sent) for b in range(blocks)
        ] and None
    )


def pipeline(sections, rows, chips, frames, upstream, acts, weights):
    channels = weights.shape[1]
    width = 128
    blocks = len(CUTS)
    bf16, f32 = jnp.bfloat16, jnp.float32
    dma = pltpu.SemaphoreType.DMA
    vmem = pl.BlockSpec(memory_space=pltpu.VMEM)
    depth = (frames + 2) * SLAB + GROUP
    reach = rows // 4
    return pl.pallas_call(
        functools.partial(pipeline_kernel, sections, rows, chips, frames),
        out_shape=(
            jax.ShapeDtypeStruct((GROUP * frames, width), bf16),
            jax.ShapeDtypeStruct((27, 2, 2, 16, channels), bf16),
        ),
        in_specs=[vmem] * 3,
        out_specs=(pl.BlockSpec(memory_space=pl.ANY),) * 2,
        scratch_shapes=[
            pltpu.VMEM((3, frames + 2, GROUP, width), bf16),
            pltpu.VMEM((3, frames + 2, GROUP, width), bf16),
            pltpu.VMEM((depth, width), bf16),
            pltpu.VMEM((depth, width), bf16),
            pltpu.VMEM((2 * chips, GROUP, PADDED), bf16),
            pltpu.VMEM((chips, GROUP, PADDED), bf16),
            pltpu.VMEM((frames, chips, GROUP, width), bf16),
            pltpu.VMEM((frames, chips, GROUP, width), bf16),
            pltpu.VMEM((channels * frames, width), f32),
            pltpu.VMEM((frames, GROUP, width), f32),
            pltpu.VMEM((frames * width, channels), bf16),
            pltpu.VMEM((DEPTH, channels), f32),
            pltpu.VMEM((GROUP * frames, width), f32),
            pltpu.VMEM((frames, GROUP, width), bf16),
            pltpu.VMEM((27, 2, 2, 16, channels), bf16),
            pltpu.VMEM((27, 2, 2, 16, channels), bf16),
            pltpu.VMEM((3, 2, reach, 2, 9, 16, width), bf16),
            pltpu.VMEM((2, reach, 9, 16, width), bf16),
            pltpu.VMEM((3, 2, 2, 9, 16, width), bf16),
            pltpu.VMEM((3, 9, 16, width), bf16),
            pltpu.VMEM((9, 2, 16, channels), bf16),
            pltpu.VMEM((GROUP * frames, width), bf16),
            dma((blocks, 3)),
            dma((blocks, 3)),
            dma((blocks, 3)),
            dma((blocks, 3)),
            dma((blocks, 3)),
            dma((blocks, chips)),
            dma((blocks, chips)),
            dma((chips,)),
            dma((chips,)),
            dma((3, 2, reach)),
            dma((3, 2, reach)),
            dma((3,)),
            dma((3,)),
            dma((3, 2, reach, 2)),
            dma((3, 2, reach, 2)),
            dma((3,)),
            dma((3,)),
            dma((rows // 2,)),
            dma((rows // 2,)),
            dma((3, 2, 2)),
            dma((3, 2, 2)),
            dma((4,)),
        ],
        compiler_params=pltpu.CompilerParams(collective_id=0, has_side_effects=True),
        name="pipeline",
    )(upstream, acts, weights)


def hand_over_kernel(grads_in, wg_in, grads_ref, wg_ref, g_held, w_held, in_sem, out_sem):
    def steps(copy):
        for n in range(9):
            taps = pl.ds(3 * n, 3)
            copy(n, wg_in.at[taps], w_held.at[taps], wg_ref.at[taps])
        copy(9, grads_in, g_held, grads_ref)

    def fetch(n, source, held, target):
        pltpu.make_async_copy(source, held, in_sem.at[n]).start()

    def pass_on(n, source, held, target):
        pltpu.make_async_copy(source, held, in_sem.at[n]).wait()
        pltpu.make_async_copy(held, target, out_sem.at[n]).start()

    def finish(n, source, held, target):
        pltpu.make_async_copy(held, target, out_sem.at[n]).wait()

    steps(fetch)
    steps(pass_on)
    steps(finish)


def hand_over(grads, kernel_sum):
    anywhere = pl.BlockSpec(memory_space=pl.ANY)
    dma = pltpu.SemaphoreType.DMA
    return pl.pallas_call(
        hand_over_kernel,
        out_shape=tuple(jax.ShapeDtypeStruct(a.shape, a.dtype) for a in (grads, kernel_sum)),
        in_specs=[anywhere] * 2,
        out_specs=(anywhere,) * 2,
        scratch_shapes=[
            pltpu.VMEM(grads.shape, grads.dtype),
            pltpu.VMEM(kernel_sum.shape, kernel_sum.dtype),
            dma((10,)),
            dma((10,)),
        ],
        name="hand_over",
    )(grads, kernel_sum)


def solution(mesh):
    sections, rows, chans = (mesh.shape[a] for a in ("section", "frame", "chan"))

    def body(upstream, acts, weights):
        group, frames, _, width = upstream.shape
        channels = acts.shape[1]
        grads, kernel_sum = pipeline(
            sections,
            rows,
            chans // 2,
            frames,
            upstream.reshape(group * frames, width),
            acts.reshape(channels * frames, width),
            weights.reshape(27 * group, channels),
        )
        grads, kernel_sum = hand_over(grads, kernel_sum)
        return grads.reshape(1, group, frames, 1, width), kernel_sum.reshape(1, 27, group, channels)

    return jax.shard_map(
        body,
        mesh=mesh,
        in_specs=(
            P("chan", None, "frame", None),
            P("section", None, None, "frame", None),
            P("section", None, "chan", None),
        ),
        out_specs=(P("section", "chan", None, "frame", None), P("section", None, "chan", None)),
        check_vma=False,
    )
```

```python
import functools

import jax
import jax.numpy as jnp
from jax import lax
from jax.experimental import pallas as pl
from jax.experimental.pallas import tpu as pltpu
from jax.sharding import PartitionSpec as P

MESH = pl.DeviceIdType.MESH
CUTS = (2, 2, 2, 2)
AHEAD = 2
CROSS = 2
GROUP = 64
SLAB = 9 * GROUP
DEPTH = 27 * GROUP
PADDED = 28 * GROUP


def remote(src, dst, send_sem, recv_sem, device):
    return pltpu.make_async_remote_copy(
        src_ref=src, dst_ref=dst, send_sem=send_sem, recv_sem=recv_sem, device_id=device, device_id_type=MESH
    )


def pipeline_kernel(
    sections, rows, chips, frames,
    up_ref, acts_ref, w_ref, grads_ref, wg_ref,
    g_own, g_par, x_own, x_par, wt, wp, part, recv, a32, slope, feat, acc, o32, gout,
    wsum, wfin, chain, short_chain, last_in, half_in, whole_in, g16,
    u_send, g_send, g_recv, f_send, f_recv, r_send, r_recv, w_send, w_recv,
    c_send, c_recv, y_send, y_recv, a_send, a_recv, b_send, b_recv, e_send, e_recv, l_send, l_recv, o_sem,
):
    channels = w_ref.shape[1]
    chans = 2 * chips
    blocks = len(CUTS)
    width = 128
    s = lax.axis_index("section")
    f = lax.axis_index("frame")
    d = lax.axis_index("chan")
    chip = d // 2
    core = d % 2
    partner = d + 1 - 2 * core

    barrier = pltpu.get_barrier_semaphore()
    peers = []
    for ds in (1, sections - 1):
        for df in (0, 1, rows - 1):
            peers.append(((s + ds) % sections, (f + df) % rows, d))
    for df in (1, rows - 1):
        peers.append((s, (f + df) % rows, d))
    peers.append((s, f, partner))
    for dq in range(1, chips):
        peers.append((s, f, ((chip + dq) % chips) * 2 + core))
    ring = rows // 2
    lanes = ring // 2
    reach = ring // 2
    h = f // ring
    z = f % ring
    across = (s, (1 - h) * ring + z, d)
    peers.append(across)
    for dz in (1, ring - 1):
        for row in (h, 1 - h):
            peers.append((s, row * ring + (z + dz) % ring, d))
    for peer in peers:
        pl.semaphore_signal(barrier, inc=1, device_id=peer, device_id_type=MESH)

    has_up = f > 0
    has_down = f < rows - 1

    for g in (g_own, g_par):
        for row in range(3):
            g[row, frames:] = jnp.zeros((2, GROUP, width), jnp.bfloat16)

        @pl.when(jnp.logical_not(has_down))
        def _():
            g[0, :frames] = jnp.zeros((frames, GROUP, width), jnp.bfloat16)

        @pl.when(jnp.logical_not(has_up))
        def _():
            g[2, :frames] = jnp.zeros((frames, GROUP, width), jnp.bfloat16)

    for x in (x_own, x_par):
        x[frames * SLAB :] = jnp.zeros((x.shape[0] - frames * SLAB, width), jnp.bfloat16)

    @pl.when(s == 0)
    def _():
        o32[...] = up_ref[...].astype(jnp.float32)
        for t in range(frames):
            g_own[1, t] = o32[pl.ds(t, GROUP, stride=frames), :].astype(jnp.bfloat16)

    for q in range(chans):
        wt[q, :, DEPTH:] = jnp.zeros((GROUP, PADDED - DEPTH), jnp.bfloat16)
    step = 2 * GROUP
    for k in range(0, DEPTH, step):
        size = min(step, DEPTH - k)
        turned = w_ref[k : k + size, :].astype(jnp.float32).T.astype(jnp.bfloat16)
        for q in range(chans):
            wt[q, :, k : k + size] = turned[q * GROUP : (q + 1) * GROUP]

    pl.semaphore_wait(barrier, len(peers))

    def frames_of(b):
        return frames - sum(CUTS[: b + 1])

    def range_of(b):
        return range(frames_of(b), frames_of(b) + CUTS[b])

    def weight_copy(q):
        return remote(wt.at[2 * q + 1 - core], wp.at[q], w_send.at[q], w_recv.at[q], (s, f, partner))

    def row_copy(src, b, slot, section, row, out_sem=g_send):
        first = frames_of(b)
        return remote(
            src,
            g_own.at[slot, pl.ds(first, CUTS[b])],
            out_sem.at[b, slot],
            g_recv.at[b, slot],
            (section, row, d),
        )

    def spread(src, b, section, centre, go):
        out_sem = g_send if centre else u_send
        if centre:
            go(row_copy(src, b, 1, section, f, out_sem))

        @pl.when(has_down)
        def _():
            go(row_copy(src, b, 2, section, (f + 1) % rows, out_sem))

        @pl.when(has_up)
        def _():
            go(row_copy(src, b, 0, section, (f + rows - 1) % rows, out_sem))

    def begin(copy):
        copy.start()

    def sent(copy):
        copy.wait_send()

    def arrived(copy):
        copy.wait_recv()

    def block_of(g, b):
        return g.at[1, pl.ds(frames_of(b), CUTS[b])]

    for q in range(chips):
        weight_copy(q).start()

    @pl.when(s == 0)
    def _():
        for b in range(blocks):
            spread(block_of(g_own, b), b, s, False, begin)

    def forward_copy(b, slot):
        first = pl.ds(frames_of(b), CUTS[b])
        return remote(
            g_own.at[slot, first], g_par.at[slot, first], f_send.at[b, slot], f_recv.at[b, slot], (s, f, partner)
        )

    def per_slot(fn):
        fn(1)
        pl.when(has_down)(lambda: fn(0))
        pl.when(has_up)(lambda: fn(2))

    def take(b):
        def one(slot):
            copy = row_copy(block_of(g_own, b), b, slot, s, f)
            if slot == 1:
                pl.when(s > 0)(lambda: copy.wait_recv())
            else:
                copy.wait_recv()
            forward_copy(b, slot).start()

        per_slot(one)

    lane = lax.broadcasted_iota(jnp.int32, (GROUP, width), 1)

    def build(g, x, t):
        for slot in range(3):
            row = g[slot, t].astype(jnp.float32)
            after = jnp.where(lane == width - 1, 0.0, pltpu.roll(row, width - 1, 1))
            before = jnp.where(lane == 0, 0.0, pltpu.roll(row, 1, 1))
            base = t * SLAB + slot * 3 * GROUP
            x[base : base + GROUP] = after.astype(jnp.bfloat16)
            x[base + GROUP : base + 2 * GROUP] = row.astype(jnp.bfloat16)
            x[base + 2 * GROUP : base + 3 * GROUP] = before.astype(jnp.bfloat16)

    def columns(x, b):
        return jnp.concatenate([x[t * SLAB : t * SLAB + PADDED] for t in range_of(b)], axis=1)

    def term_copy(b, q):
        at = pl.ds(frames_of(b), CUTS[b])
        return remote(
            part.at[at, q], recv.at[at, chip], r_send.at[b, q], r_recv.at[b, chip], (s, f, 2 * q + core)
        )

    def term_arrival(b, q):
        at = pl.ds(frames_of(b), CUTS[b])
        return remote(part.at[at, q], recv.at[at, q], r_send.at[b, q], r_recv.at[b, q], (s, f, 2 * q + core))

    ways = (1, -1)
    splits = (pl.ds(0, 5), pl.ds(5, 4))

    def along(way, side=0):
        row = 1 - h if side else h
        return (s, row * ring + (z + way + ring) % ring, d)

    def place(offset):
        return (z + offset + 2 * ring) % ring

    def piece(ref, first, count, half, owner):
        columns = pl.ds(pl.multiple_of((owner % lanes) * width, width), width)
        return ref.at[pl.ds(first, count), half, owner // lanes, :, columns]

    def chain_copy(p, e, k):
        if k == 0:
            src = piece(wsum, 9 * p, 9, e, place(ways[e] * reach))
            dst = chain.at[p, e, 0, e]
        else:
            src, dst = chain.at[p, e, k - 1], chain.at[p, e, k]
        return remote(src, dst, c_send.at[p, e, k], c_recv.at[p, e, k], along(ways[e]))

    def own_term(p, half, offset):
        return piece(wsum, 9 * p, 9, half, place(offset))[...].astype(jnp.float32)

    def chain_step(p, k):
        for e, way in enumerate(ways):
            chain_copy(p, e, k - 1).wait_recv()
            for half in range(2):
                term = own_term(p, half, way * (reach - k))
                if k > 1 or half == e:
                    term = term + chain[p, e, k - 1, half].astype(jnp.float32)
                chain[p, e, k - 1, half] = term.astype(jnp.bfloat16)
            if k < reach - 1:
                chain_copy(p, e, k).start()
            else:
                for side in range(2):
                    last_copy(p, e, side).start()

    def last_copy(p, e, side):
        half = 1 - h if side else h
        return remote(
            chain.at[p, e, reach - 2, half],
            last_in.at[p, e, side],
            l_send.at[p, e, side],
            l_recv.at[p, e, side],
            along(ways[e], side),
        )

    def half_copy(p):
        return remote(
            piece(wsum, 9 * p, 9, 1 - h, z), half_in.at[p], y_send.at[p], y_recv.at[p], across
        )

    def chain_end(p):
        half_copy(p).wait_recv()
        total = own_term(p, h, 0) + half_in[p].astype(jnp.float32)
        for side in range(2):
            for e in range(2):
                last_copy(p, e, side).wait_recv()
                total = total + last_in[p, e, side].astype(jnp.float32)
        piece(wfin, 9 * p, 9, h, z)[...] = total.astype(jnp.bfloat16)
        for side in range(2):
            for e in range(2):
                first_copy(p, e, side).start()
        share_copy(p, h).start()

    def first_copy(p, e, side):
        at = piece(wfin, 9 * p, 9, h, z)
        slot = 1 - h if side else h
        return remote(at, at, a_send.at[p, e, 0, slot], a_recv.at[p, e, 0, h], along(ways[e], side))

    def share_copy(p, half):
        at = piece(wfin, 9 * p, 9, half, z)
        return remote(at, at, b_send.at[p], b_recv.at[p], across)

    def gather_copy(p, e, k, half, arrival=False):
        at = piece(wfin, 9 * p, 9, half, place(-ways[e] * (k + 1 if arrival else k)))
        return remote(at, at, a_send.at[p, e, k, half], a_recv.at[p, e, k, half], along(ways[e]))

    def gather_step(p, k):
        for half in (h, 1 - h):
            for e in range(2):
                gather_copy(p, e, k - 1, half, True).wait_recv()
                if k < reach - 1:
                    gather_copy(p, e, k, half).start()
        if k == reach - 1:
            for e in range(2):
                gather_copy(p, e, k, e).start()

    def gather_end(p):
        share_copy(p, 1 - h).wait_recv()
        for e in range(2):
            gather_copy(p, e, reach - 1, e, True).wait_recv()

    def whole_copy():
        return remote(wsum.at[pl.ds(9 * CROSS, 9), 1 - h], whole_in, y_send.at[CROSS], y_recv.at[CROSS], across)

    def short_copy(e, k):
        if k == 0:
            taps = splits[e]
            src = piece(wsum, 9 * CROSS + taps.start, taps.size, h, place(ways[e] * reach))
            dst = short_chain.at[e, 0, taps]
        else:
            src, dst = short_chain.at[e, k - 1], short_chain.at[e, k]
        return remote(src, dst, c_send.at[CROSS, e, k], c_recv.at[CROSS, e, k], along(ways[e]))

    def whole_end():
        whole_copy().wait_recv()
        for n in range(9):
            both = wsum[9 * CROSS + n, h].astype(jnp.float32) + whole_in[n].astype(jnp.float32)
            wsum[9 * CROSS + n, h] = both.astype(jnp.bfloat16)
        for e in range(2):
            short_copy(e, 0).start()

    def short_step(k):
        for e, way in enumerate(ways):
            short_copy(e, k - 1).wait_recv()
            for n in range(9):
                term = piece(wsum, 9 * CROSS + n, 1, h, place(way * (reach - k)))[...].astype(jnp.float32)
                low = splits[e].start
                if k > 1 or low <= n < low + splits[e].size:
                    term = term + short_chain[e, k - 1, n].astype(jnp.float32)
                short_chain[e, k - 1, n] = term[0].astype(jnp.bfloat16)
            short_copy(e, k).start()

    def cross_copy(n, owner, half):
        at = piece(wfin, 9 * CROSS, 9, half, owner)
        return remote(at, at, e_send.at[n], e_recv.at[n], across)

    def spread_copy(e, k, arrival=False):
        owner = place(-ways[e] * (k + 1 if arrival else k))
        first, count = (splits[e].start, splits[e].size) if k == reach - 1 else (0, 9)
        at = piece(wfin, 9 * CROSS + first, count, h, owner)
        return remote(at, at, a_send.at[CROSS, e, k, 0], a_recv.at[CROSS, e, k, 0], along(ways[e]))

    def short_end():
        final = own_term(CROSS, h, 0)
        for e in range(2):
            short_copy(e, reach - 1).wait_recv()
            final = final + short_chain[e, reach - 1].astype(jnp.float32)
        piece(wfin, 9 * CROSS, 9, h, z)[...] = final.astype(jnp.bfloat16)
        for e in range(2):
            spread_copy(e, 0).start()
        cross_copy(0, z, h).start()

    def spread_step(k):
        for e in range(2):
            spread_copy(e, k - 1, True).wait_recv()
            spread_copy(e, k).start()
            cross_copy(1 + 2 * (k - 1) + e, place(-ways[e] * k), h).start()

    def spread_end():
        for e in range(2):
            spread_copy(e, reach - 1, True).wait_recv()
        cross_copy(ring - 1, place(reach), h).start()

    def cross_all(half, go):
        go(cross_copy(0, z, half))
        for k in range(1, reach):
            for e in range(2):
                go(cross_copy(1 + 2 * (k - 1) + e, place(-ways[e] * k), half))
        go(cross_copy(ring - 1, place(reach), half))

    later = tuple(p for p in (2, 1, 0) if p != CROSS)

    def sum_begin(p):
        if p == CROSS:
            whole_copy().start()
        else:
            for e in range(2):
                chain_copy(p, e, 0).start()
            half_copy(p).start()

    def sum_finish(between):
        one, two = later
        for k in range(1, reach):
            chain_step(one, k)
            if k == 1:
                between(0)
            if k > 1:
                short_step(k - 1)
            chain_step(two, k)
            if k == 1:
                whole_end()
            between(k)
        chain_end(one)
        short_step(reach - 1)
        chain_end(two)
        short_end()
        for k in range(1, reach):
            gather_step(one, k)
            spread_step(k)
            gather_step(two, k)
        gather_end(one)
        out_copy(one).start()
        spread_end()
        gather_end(two)
        out_copy(two).start()
        cross_all(1 - h, arrived)
        out_copy(CROSS).start()

    def out_copy(p):
        taps = pl.ds(9 * p, 9)
        return pltpu.make_async_copy(wfin.at[taps], wg_ref.at[taps], o_sem.at[p])

    def grads_copy():
        return pltpu.make_async_copy(g16, grads_ref, o_sem.at[3])

    def grads_out():
        g16[...] = o32[...].astype(jnp.bfloat16)
        grads_copy().start()

    def sum_sent():
        whole_copy().wait_send()
        for e in range(2):
            for k in range(reach):
                short_copy(e, k).wait_send()
                spread_copy(e, k).wait_send()
        cross_all(h, sent)
        for p in later:
            half_copy(p).wait_send()
            share_copy(p, h).wait_send()
            for e in range(2):
                for side in range(2):
                    last_copy(p, e, side).wait_send()
                    first_copy(p, e, side).wait_send()
                for k in range(reach - 1):
                    chain_copy(p, e, k).wait_send()
                for k in range(1, reach):
                    for half in range(2) if k < reach - 1 else (e,):
                        gather_copy(p, e, k, half).wait_send()

    hops = sorted(range(1, chips), key=lambda o: -min(o, chips - o))

    last = sections - 1
    final = blocks - 1

    def prepare():
        a32[...] = acts_ref[...].astype(jnp.float32)
        for t in range(frames):
            own = a32[pl.ds(d * (GROUP * frames) + t, GROUP, stride=frames), :]
            logistic = 1.0 / (1.0 + jnp.exp(-own))
            slope[t] = logistic * (1.0 + own * (1.0 - logistic))
            for q in range(0, channels, step):
                values = a32[pl.ds(q * frames + t, step, stride=frames), :]
                values = values / (1.0 + jnp.exp(-values))
                feat[t * width : (t + 1) * width, q : q + step] = values.T.astype(jnp.bfloat16)

    def back_terms(b):
        lhs = jnp.concatenate([wt[2 * q + core] for q in range(chips)], axis=0)
        total = jnp.dot(lhs, columns(x_own, b), preferred_element_type=jnp.float32)
        if b == 0:
            for q in range(chips):
                weight_copy(q).wait_recv()
        per_slot(lambda slot: forward_copy(b, slot).wait_recv())
        for t in range_of(b):
            build(g_par, x_par, t)
        lhs = jnp.concatenate([wp[q] for q in range(chips)], axis=0)
        total = total + jnp.dot(lhs, columns(x_par, b), preferred_element_type=jnp.float32)
        for n, t in enumerate(range_of(b)):
            for q in range(chips):
                block = total[q * GROUP : (q + 1) * GROUP, n * width : (n + 1) * width]
                part[t, q] = block.astype(jnp.bfloat16)
        for o in hops:
            term_copy(b, (chip + o) % chips).start()

    def kernel_terms(b):
        for k in range(3):
            at = slice(k * SLAB, (k + 1) * SLAB)
            source = [t for t in range_of(b) if t >= k]
            add = None
            if source:
                lhs = jnp.concatenate([x_own[t * SLAB : (t + 1) * SLAB] for t in source], axis=1)
                cells = slice((source[0] - k) * width, (source[-1] - k + 1) * width)
                add = jnp.dot(lhs, feat[cells, :], preferred_element_type=jnp.float32)
                if b > 0:
                    add = add + acc[at]
            if source and source[0] == k:
                wsum[9 * k : 9 * k + 9] = add.astype(jnp.bfloat16).reshape(9, 2, 2, 16, channels)
            elif source:
                acc[at] = add

    def update(b):
        for o in reversed(hops):
            term_arrival(b, (chip + o) % chips).wait_recv()
        for t in range_of(b):
            back = part[t, chip].astype(jnp.float32)
            for o in hops:
                back = back + recv[t, (chip + o) % chips].astype(jnp.float32)
            new = (g_own[1, t].astype(jnp.float32) + slope[t] * back).astype(jnp.bfloat16)
            gout[t] = new
            o32[pl.ds(t, GROUP, stride=frames), :] = new.astype(jnp.float32)
        part_out = gout.at[pl.ds(frames_of(b), CUTS[b])]
        pl.when(s < last)(lambda: spread(part_out, b, (s + 1) % sections, True, begin))

    def complete(b):
        return [k for k in (2, 1, 0) if k in range_of(b)]

    pl.when(s > 0)(prepare)
    for b in range(blocks):
        take(b)
        for t in range_of(b):
            build(g_own, x_own, t)

        @pl.when(s == last)
        def _():
            kernel_terms(b)
            for k in complete(b):
                sum_begin(k)

        if b < final:
            back_terms(b)
        else:
            pl.when(s < last)(lambda: back_terms(final))
        if b == 0:
            pl.when(s == 0)(prepare)
        if b >= AHEAD - 1:
            pl.when(s < last)(lambda: update(b - AHEAD + 1))

    @pl.when(s < last)
    def _():
        for b in range(blocks - AHEAD + 1, blocks):
            update(b)
        grads_out()
        for b in range(blocks):
            kernel_terms(b)
            for k in complete(b):
                sum_begin(k)

    def between(k):
        @pl.when(s == last)
        def _():
            if k == 0:
                back_terms(final)
            if k == min(2, reach - 1):
                for b in range(blocks):
                    update(b)
                grads_out()

    sum_finish(between)
    sum_sent()
    for p in range(3):
        out_copy(p).wait()
    grads_copy().wait()

    for q in range(chips):
        weight_copy(q).wait_send()

    @pl.when(s == 0)
    def _():
        for b in range(blocks):
            spread(block_of(g_own, b), b, s, False, sent)

    for b in range(blocks):
        per_slot(lambda slot: forward_copy(b, slot).wait_send())
        for o in hops:
            term_copy(b, (chip + o) % chips).wait_send()

    pl.when(s < sections - 1)(
        lambda: [
            spread(gout.at[pl.ds(frames_of(b), CUTS[b])], b, (s + 1) % sections, True, sent) for b in range(blocks)
        ] and None
    )


def pipeline(sections, rows, chips, frames, upstream, acts, weights):
    channels = weights.shape[1]
    width = 128
    blocks = len(CUTS)
    bf16, f32 = jnp.bfloat16, jnp.float32
    dma = pltpu.SemaphoreType.DMA
    vmem = pl.BlockSpec(memory_space=pltpu.VMEM)
    depth = (frames + 2) * SLAB + GROUP
    reach = rows // 4
    return pl.pallas_call(
        functools.partial(pipeline_kernel, sections, rows, chips, frames),
        out_shape=(
            jax.ShapeDtypeStruct((GROUP * frames, width), bf16),
            jax.ShapeDtypeStruct((27, 2, 2, 16, channels), bf16),
        ),
        in_specs=[vmem] * 3,
        out_specs=(pl.BlockSpec(memory_space=pl.ANY),) * 2,
        scratch_shapes=[
            pltpu.VMEM((3, frames + 2, GROUP, width), bf16),
            pltpu.VMEM((3, frames + 2, GROUP, width), bf16),
            pltpu.VMEM((depth, width), bf16),
            pltpu.VMEM((depth, width), bf16),
            pltpu.VMEM((2 * chips, GROUP, PADDED), bf16),
            pltpu.VMEM((chips, GROUP, PADDED), bf16),
            pltpu.VMEM((frames, chips, GROUP, width), bf16),
            pltpu.VMEM((frames, chips, GROUP, width), bf16),
            pltpu.VMEM((channels * frames, width), f32),
            pltpu.VMEM((frames, GROUP, width), f32),
            pltpu.VMEM((frames * width, channels), bf16),
            pltpu.VMEM((DEPTH, channels), f32),
            pltpu.VMEM((GROUP * frames, width), f32),
            pltpu.VMEM((frames, GROUP, width), bf16),
            pltpu.VMEM((27, 2, 2, 16, channels), bf16),
            pltpu.VMEM((27, 2, 2, 16, channels), bf16),
            pltpu.VMEM((3, 2, reach, 2, 9, 16, width), bf16),
            pltpu.VMEM((2, reach, 9, 16, width), bf16),
            pltpu.VMEM((3, 2, 2, 9, 16, width), bf16),
            pltpu.VMEM((3, 9, 16, width), bf16),
            pltpu.VMEM((9, 2, 16, channels), bf16),
            pltpu.VMEM((GROUP * frames, width), bf16),
            dma((blocks, 3)),
            dma((blocks, 3)),
            dma((blocks, 3)),
            dma((blocks, 3)),
            dma((blocks, 3)),
            dma((blocks, chips)),
            dma((blocks, chips)),
            dma((chips,)),
            dma((chips,)),
            dma((3, 2, reach)),
            dma((3, 2, reach)),
            dma((3,)),
            dma((3,)),
            dma((3, 2, reach, 2)),
            dma((3, 2, reach, 2)),
            dma((3,)),
            dma((3,)),
            dma((rows // 2,)),
            dma((rows // 2,)),
            dma((3, 2, 2)),
            dma((3, 2, 2)),
            dma((4,)),
        ],
        compiler_params=pltpu.CompilerParams(collective_id=0, has_side_effects=True),
        name="pipeline",
    )(upstream, acts, weights)


def hand_over_kernel(grads_in, wg_in, grads_ref, wg_ref, g_held, w_held, in_sem, out_sem):
    def steps(copy):
        for n in range(9):
            taps = pl.ds(3 * n, 3)
            copy(n, wg_in.at[taps], w_held.at[taps], wg_ref.at[taps])
        copy(9, grads_in, g_held, grads_ref)

    def fetch(n, source, held, target):
        pltpu.make_async_copy(source, held, in_sem.at[n]).start()

    def pass_on(n, source, held, target):
        pltpu.make_async_copy(source, held, in_sem.at[n]).wait()
        pltpu.make_async_copy(held, target, out_sem.at[n]).start()

    def finish(n, source, held, target):
        pltpu.make_async_copy(held, target, out_sem.at[n]).wait()

    steps(fetch)
    steps(pass_on)
    steps(finish)


def hand_over(grads, kernel_sum):
    anywhere = pl.BlockSpec(memory_space=pl.ANY)
    dma = pltpu.SemaphoreType.DMA
    return pl.pallas_call(
        hand_over_kernel,
        out_shape=tuple(jax.ShapeDtypeStruct(a.shape, a.dtype) for a in (grads, kernel_sum)),
        in_specs=[anywhere] * 2,
        out_specs=(anywhere,) * 2,
        scratch_shapes=[
            pltpu.VMEM(grads.shape, grads.dtype),
            pltpu.VMEM(kernel_sum.shape, kernel_sum.dtype),
            dma((10,)),
            dma((10,)),
        ],
        name="hand_over",
    )(grads, kernel_sum)


def solution(mesh):
    sections, rows, chans = (mesh.shape[a] for a in ("section", "frame", "chan"))

    def body(upstream, acts, weights):
        group, frames, _, width = upstream.shape
        channels = acts.shape[1]
        grads, kernel_sum = pipeline(
            sections,
            rows,
            chans // 2,
            frames,
            upstream.reshape(group * frames, width),
            acts.reshape(channels * frames, width),
            weights.reshape(27 * group, channels),
        )
        grads, kernel_sum = hand_over(grads, kernel_sum)
        return grads.reshape(1, group, frames, 1, width), kernel_sum.reshape(1, 27, group, channels)

    return jax.shard_map(
        body,
        mesh=mesh,
        in_specs=(
            P("chan", None, "frame", None),
            P("section", None, None, "frame", None),
            P("section", None, "chan", None),
        ),
        out_specs=(P("section", "chan", None, "frame", None), P("section", None, "chan", None)),
        check_vma=False,
    )
```

```python
import functools

import jax
import jax.numpy as jnp
from jax import lax
from jax.experimental import pallas as pl
from jax.experimental.pallas import tpu as pltpu
from jax.sharding import PartitionSpec as P

MESH = pl.DeviceIdType.MESH
CUTS = (2, 2, 2, 2)
AHEAD = 2
CROSS = 2
GROUP = 64
SLAB = 9 * GROUP
DEPTH = 27 * GROUP
PADDED = 28 * GROUP


def remote(src, dst, send_sem, recv_sem, device):
    return pltpu.make_async_remote_copy(
        src_ref=src, dst_ref=dst, send_sem=send_sem, recv_sem=recv_sem, device_id=device, device_id_type=MESH
    )


def pipeline_kernel(
    sections, rows, chips, frames,
    up_ref, acts_ref, w_ref, grads_ref, wg_ref,
    g_own, g_par, x_own, x_par, wt, wp, part, recv, a32, slope, feat, acc, o32, gout,
    wsum, wfin, chain, short_chain, last_in, half_in, whole_in, g16,
    u_send, g_send, g_recv, f_send, f_recv, r_send, r_recv, w_send, w_recv,
    c_send, c_recv, y_send, y_recv, a_send, a_recv, b_send, b_recv, e_send, e_recv, l_send, l_recv, o_sem,
):
    channels = w_ref.shape[1]
    chans = 2 * chips
    blocks = len(CUTS)
    width = 128
    s = lax.axis_index("section")
    f = lax.axis_index("frame")
    d = lax.axis_index("chan")
    chip = d // 2
    core = d % 2
    partner = d + 1 - 2 * core

    barrier = pltpu.get_barrier_semaphore()
    peers = []
    for ds in (1, sections - 1):
        for df in (0, 1, rows - 1):
            peers.append(((s + ds) % sections, (f + df) % rows, d))
    for df in (1, rows - 1):
        peers.append((s, (f + df) % rows, d))
    peers.append((s, f, partner))
    for dq in range(1, chips):
        peers.append((s, f, ((chip + dq) % chips) * 2 + core))
    ring = rows // 2
    lanes = ring // 2
    reach = ring // 2
    h = f // ring
    z = f % ring
    across = (s, (1 - h) * ring + z, d)
    peers.append(across)
    for dz in (1, ring - 1):
        for row in (h, 1 - h):
            peers.append((s, row * ring + (z + dz) % ring, d))
    for peer in peers:
        pl.semaphore_signal(barrier, inc=1, device_id=peer, device_id_type=MESH)

    has_up = f > 0
    has_down = f < rows - 1

    for g in (g_own, g_par):
        for row in range(3):
            g[row, frames:] = jnp.zeros((2, GROUP, width), jnp.bfloat16)

        @pl.when(jnp.logical_not(has_down))
        def _():
            g[0, :frames] = jnp.zeros((frames, GROUP, width), jnp.bfloat16)

        @pl.when(jnp.logical_not(has_up))
        def _():
            g[2, :frames] = jnp.zeros((frames, GROUP, width), jnp.bfloat16)

    for x in (x_own, x_par):
        x[frames * SLAB :] = jnp.zeros((x.shape[0] - frames * SLAB, width), jnp.bfloat16)

    @pl.when(s == 0)
    def _():
        o32[...] = up_ref[...].astype(jnp.float32)
        for t in range(frames):
            g_own[1, t] = o32[pl.ds(t, GROUP, stride=frames), :].astype(jnp.bfloat16)

    for q in range(chans):
        wt[q, :, DEPTH:] = jnp.zeros((GROUP, PADDED - DEPTH), jnp.bfloat16)
    step = 2 * GROUP
    for k in range(0, DEPTH, step):
        size = min(step, DEPTH - k)
        turned = w_ref[k : k + size, :].astype(jnp.float32).T.astype(jnp.bfloat16)
        for q in range(chans):
            wt[q, :, k : k + size] = turned[q * GROUP : (q + 1) * GROUP]

    pl.semaphore_wait(barrier, len(peers))

    def frames_of(b):
        return frames - sum(CUTS[: b + 1])

    def range_of(b):
        return range(frames_of(b), frames_of(b) + CUTS[b])

    def weight_copy(q):
        return remote(wt.at[2 * q + 1 - core], wp.at[q], w_send.at[q], w_recv.at[q], (s, f, partner))

    def row_copy(src, b, slot, section, row, out_sem=g_send):
        first = frames_of(b)
        return remote(
            src,
            g_own.at[slot, pl.ds(first, CUTS[b])],
            out_sem.at[b, slot],
            g_recv.at[b, slot],
            (section, row, d),
        )

    def spread(src, b, section, centre, go):
        out_sem = g_send if centre else u_send
        if centre:
            go(row_copy(src, b, 1, section, f, out_sem))

        @pl.when(has_down)
        def _():
            go(row_copy(src, b, 2, section, (f + 1) % rows, out_sem))

        @pl.when(has_up)
        def _():
            go(row_copy(src, b, 0, section, (f + rows - 1) % rows, out_sem))

    def begin(copy):
        copy.start()

    def sent(copy):
        copy.wait_send()

    def arrived(copy):
        copy.wait_recv()

    def block_of(g, b):
        return g.at[1, pl.ds(frames_of(b), CUTS[b])]

    for q in range(chips):
        weight_copy(q).start()

    @pl.when(s == 0)
    def _():
        for b in range(blocks):
            spread(block_of(g_own, b), b, s, False, begin)

    def forward_copy(b, slot):
        first = pl.ds(frames_of(b), CUTS[b])
        return remote(
            g_own.at[slot, first], g_par.at[slot, first], f_send.at[b, slot], f_recv.at[b, slot], (s, f, partner)
        )

    def per_slot(fn):
        fn(1)
        pl.when(has_down)(lambda: fn(0))
        pl.when(has_up)(lambda: fn(2))

    def take(b):
        def one(slot):
            copy = row_copy(block_of(g_own, b), b, slot, s, f)
            if slot == 1:
                pl.when(s > 0)(lambda: copy.wait_recv())
            else:
                copy.wait_recv()
            forward_copy(b, slot).start()

        per_slot(one)

    lane = lax.broadcasted_iota(jnp.int32, (GROUP, width), 1)

    def build(g, x, t):
        for slot in range(3):
            row = g[slot, t].astype(jnp.float32)
            after = jnp.where(lane == width - 1, 0.0, pltpu.roll(row, width - 1, 1))
            before = jnp.where(lane == 0, 0.0, pltpu.roll(row, 1, 1))
            base = t * SLAB + slot * 3 * GROUP
            x[base : base + GROUP] = after.astype(jnp.bfloat16)
            x[base + GROUP : base + 2 * GROUP] = row.astype(jnp.bfloat16)
            x[base + 2 * GROUP : base + 3 * GROUP] = before.astype(jnp.bfloat16)

    def columns(x, b):
        return jnp.concatenate([x[t * SLAB : t * SLAB + PADDED] for t in range_of(b)], axis=1)

    def term_copy(b, q):
        at = pl.ds(frames_of(b), CUTS[b])
        return remote(
            part.at[at, q], recv.at[at, chip], r_send.at[b, q], r_recv.at[b, chip], (s, f, 2 * q + core)
        )

    def term_arrival(b, q):
        at = pl.ds(frames_of(b), CUTS[b])
        return remote(part.at[at, q], recv.at[at, q], r_send.at[b, q], r_recv.at[b, q], (s, f, 2 * q + core))

    ways = (1, -1)
    splits = (pl.ds(0, 5), pl.ds(5, 4))

    def along(way, side=0):
        row = 1 - h if side else h
        return (s, row * ring + (z + way + ring) % ring, d)

    def place(offset):
        return (z + offset + 2 * ring) % ring

    def piece(ref, first, count, half, owner):
        columns = pl.ds(pl.multiple_of((owner % lanes) * width, width), width)
        return ref.at[pl.ds(first, count), half, owner // lanes, :, columns]

    def chain_copy(p, e, k):
        if k == 0:
            src = piece(wsum, 9 * p, 9, e, place(ways[e] * reach))
            dst = chain.at[p, e, 0, e]
        else:
            src, dst = chain.at[p, e, k - 1], chain.at[p, e, k]
        return remote(src, dst, c_send.at[p, e, k], c_recv.at[p, e, k], along(ways[e]))

    def own_term(p, half, offset):
        return piece(wsum, 9 * p, 9, half, place(offset))[...].astype(jnp.float32)

    def chain_step(p, k):
        for e, way in enumerate(ways):
            chain_copy(p, e, k - 1).wait_recv()
            for half in range(2):
                term = own_term(p, half, way * (reach - k))
                if k > 1 or half == e:
                    term = term + chain[p, e, k - 1, half].astype(jnp.float32)
                chain[p, e, k - 1, half] = term.astype(jnp.bfloat16)
            if k < reach - 1:
                chain_copy(p, e, k).start()
            else:
                for side in range(2):
                    last_copy(p, e, side).start()

    def last_copy(p, e, side):
        half = 1 - h if side else h
        return remote(
            chain.at[p, e, reach - 2, half],
            last_in.at[p, e, side],
            l_send.at[p, e, side],
            l_recv.at[p, e, side],
            along(ways[e], side),
        )

    def half_copy(p):
        return remote(
            piece(wsum, 9 * p, 9, 1 - h, z), half_in.at[p], y_send.at[p], y_recv.at[p], across
        )

    def chain_end(p):
        half_copy(p).wait_recv()
        total = own_term(p, h, 0) + half_in[p].astype(jnp.float32)
        for side in range(2):
            for e in range(2):
                last_copy(p, e, side).wait_recv()
                total = total + last_in[p, e, side].astype(jnp.float32)
        piece(wfin, 9 * p, 9, h, z)[...] = total.astype(jnp.bfloat16)
        for side in range(2):
            for e in range(2):
                first_copy(p, e, side).start()
        share_copy(p, h).start()

    def first_copy(p, e, side):
        at = piece(wfin, 9 * p, 9, h, z)
        slot = 1 - h if side else h
        return remote(at, at, a_send.at[p, e, 0, slot], a_recv.at[p, e, 0, h], along(ways[e], side))

    def share_copy(p, half):
        at = piece(wfin, 9 * p, 9, half, z)
        return remote(at, at, b_send.at[p], b_recv.at[p], across)

    def gather_copy(p, e, k, half, arrival=False):
        at = piece(wfin, 9 * p, 9, half, place(-ways[e] * (k + 1 if arrival else k)))
        return remote(at, at, a_send.at[p, e, k, half], a_recv.at[p, e, k, half], along(ways[e]))

    def gather_step(p, k):
        for half in (h, 1 - h):
            for e in range(2):
                gather_copy(p, e, k - 1, half, True).wait_recv()
                if k < reach - 1:
                    gather_copy(p, e, k, half).start()
        if k == reach - 1:
            for e in range(2):
                gather_copy(p, e, k, e).start()

    def gather_end(p):
        share_copy(p, 1 - h).wait_recv()
        for e in range(2):
            gather_copy(p, e, reach - 1, e, True).wait_recv()

    def whole_copy():
        return remote(wsum.at[pl.ds(9 * CROSS, 9), 1 - h], whole_in, y_send.at[CROSS], y_recv.at[CROSS], across)

    def short_copy(e, k):
        if k == 0:
            taps = splits[e]
            src = piece(wsum, 9 * CROSS + taps.start, taps.size, h, place(ways[e] * reach))
            dst = short_chain.at[e, 0, taps]
        else:
            src, dst = short_chain.at[e, k - 1], short_chain.at[e, k]
        return remote(src, dst, c_send.at[CROSS, e, k], c_recv.at[CROSS, e, k], along(ways[e]))

    def whole_end():
        whole_copy().wait_recv()
        for n in range(9):
            both = wsum[9 * CROSS + n, h].astype(jnp.float32) + whole_in[n].astype(jnp.float32)
            wsum[9 * CROSS + n, h] = both.astype(jnp.bfloat16)
        for e in range(2):
            short_copy(e, 0).start()

    def short_step(k):
        for e, way in enumerate(ways):
            short_copy(e, k - 1).wait_recv()
            for n in range(9):
                term = piece(wsum, 9 * CROSS + n, 1, h, place(way * (reach - k)))[...].astype(jnp.float32)
                low = splits[e].start
                if k > 1 or low <= n < low + splits[e].size:
                    term = term + short_chain[e, k - 1, n].astype(jnp.float32)
                short_chain[e, k - 1, n] = term[0].astype(jnp.bfloat16)
            short_copy(e, k).start()

    def cross_copy(n, owner, half):
        at = piece(wfin, 9 * CROSS, 9, half, owner)
        return remote(at, at, e_send.at[n], e_recv.at[n], across)

    def spread_copy(e, k, arrival=False):
        owner = place(-ways[e] * (k + 1 if arrival else k))
        first, count = (splits[e].start, splits[e].size) if k == reach - 1 else (0, 9)
        at = piece(wfin, 9 * CROSS + first, count, h, owner)
        return remote(at, at, a_send.at[CROSS, e, k, 0], a_recv.at[CROSS, e, k, 0], along(ways[e]))

    def short_end():
        final = own_term(CROSS, h, 0)
        for e in range(2):
            short_copy(e, reach - 1).wait_recv()
            final = final + short_chain[e, reach - 1].astype(jnp.float32)
        piece(wfin, 9 * CROSS, 9, h, z)[...] = final.astype(jnp.bfloat16)
        for e in range(2):
            spread_copy(e, 0).start()
        cross_copy(0, z, h).start()

    def spread_step(k):
        for e in range(2):
            spread_copy(e, k - 1, True).wait_recv()
            spread_copy(e, k).start()
            cross_copy(1 + 2 * (k - 1) + e, place(-ways[e] * k), h).start()

    def spread_end():
        for e in range(2):
            spread_copy(e, reach - 1, True).wait_recv()
        cross_copy(ring - 1, place(reach), h).start()

    def cross_all(half, go):
        go(cross_copy(0, z, half))
        for k in range(1, reach):
            for e in range(2):
                go(cross_copy(1 + 2 * (k - 1) + e, place(-ways[e] * k), half))
        go(cross_copy(ring - 1, place(reach), half))

    later = tuple(p for p in (2, 1, 0) if p != CROSS)

    def sum_begin(p):
        if p == CROSS:
            whole_copy().start()
        else:
            for e in range(2):
                chain_copy(p, e, 0).start()
            half_copy(p).start()

    def sum_finish(between):
        one, two = later
        for k in range(1, reach):
            chain_step(one, k)
            if k == 1:
                between(0)
            if k > 1:
                short_step(k - 1)
            chain_step(two, k)
            if k == 1:
                whole_end()
            between(k)
        chain_end(one)
        short_step(reach - 1)
        chain_end(two)
        short_end()
        for k in range(1, reach):
            gather_step(one, k)
            spread_step(k)
            gather_step(two, k)
        gather_end(one)
        out_copy(one).start()
        spread_end()
        gather_end(two)
        out_copy(two).start()
        cross_all(1 - h, arrived)
        out_copy(CROSS).start()

    def out_copy(p):
        taps = pl.ds(9 * p, 9)
        return pltpu.make_async_copy(wfin.at[taps], wg_ref.at[taps], o_sem.at[p])

    def grads_copy():
        return pltpu.make_async_copy(g16, grads_ref, o_sem.at[3])

    def grads_out():
        g16[...] = o32[...].astype(jnp.bfloat16)
        grads_copy().start()

    def sum_sent():
        whole_copy().wait_send()
        for e in range(2):
            for k in range(reach):
                short_copy(e, k).wait_send()
                spread_copy(e, k).wait_send()
        cross_all(h, sent)
        for p in later:
            half_copy(p).wait_send()
            share_copy(p, h).wait_send()
            for e in range(2):
                for side in range(2):
                    last_copy(p, e, side).wait_send()
                    first_copy(p, e, side).wait_send()
                for k in range(reach - 1):
                    chain_copy(p, e, k).wait_send()
                for k in range(1, reach):
                    for half in range(2) if k < reach - 1 else (e,):
                        gather_copy(p, e, k, half).wait_send()

    hops = sorted(range(1, chips), key=lambda o: -min(o, chips - o))

    last = sections - 1
    final = blocks - 1

    def prepare():
        a32[...] = acts_ref[...].astype(jnp.float32)
        for t in range(frames):
            own = a32[pl.ds(d * (GROUP * frames) + t, GROUP, stride=frames), :]
            logistic = 1.0 / (1.0 + jnp.exp(-own))
            slope[t] = logistic * (1.0 + own * (1.0 - logistic))
            for q in range(0, channels, step):
                values = a32[pl.ds(q * frames + t, step, stride=frames), :]
                values = values / (1.0 + jnp.exp(-values))
                feat[t * width : (t + 1) * width, q : q + step] = values.T.astype(jnp.bfloat16)

    def back_terms(b):
        lhs = jnp.concatenate([wt[2 * q + core] for q in range(chips)], axis=0)
        total = jnp.dot(lhs, columns(x_own, b), preferred_element_type=jnp.float32)
        if b == 0:
            for q in range(chips):
                weight_copy(q).wait_recv()
        per_slot(lambda slot: forward_copy(b, slot).wait_recv())
        for t in range_of(b):
            build(g_par, x_par, t)
        lhs = jnp.concatenate([wp[q] for q in range(chips)], axis=0)
        total = total + jnp.dot(lhs, columns(x_par, b), preferred_element_type=jnp.float32)
        for n, t in enumerate(range_of(b)):
            for q in range(chips):
                block = total[q * GROUP : (q + 1) * GROUP, n * width : (n + 1) * width]
                part[t, q] = block.astype(jnp.bfloat16)
        for o in hops:
            term_copy(b, (chip + o) % chips).start()

    def kernel_terms(b):
        for k in range(3):
            at = slice(k * SLAB, (k + 1) * SLAB)
            source = [t for t in range_of(b) if t >= k]
            add = None
            if source:
                lhs = jnp.concatenate([x_own[t * SLAB : (t + 1) * SLAB] for t in source], axis=1)
                cells = slice((source[0] - k) * width, (source[-1] - k + 1) * width)
                add = jnp.dot(lhs, feat[cells, :], preferred_element_type=jnp.float32)
                if b > 0:
                    add = add + acc[at]
            if source and source[0] == k:
                wsum[9 * k : 9 * k + 9] = add.astype(jnp.bfloat16).reshape(9, 2, 2, 16, channels)
            elif source:
                acc[at] = add

    def update(b):
        for o in reversed(hops):
            term_arrival(b, (chip + o) % chips).wait_recv()
        for t in range_of(b):
            back = part[t, chip].astype(jnp.float32)
            for o in hops:
                back = back + recv[t, (chip + o) % chips].astype(jnp.float32)
            new = (g_own[1, t].astype(jnp.float32) + slope[t] * back).astype(jnp.bfloat16)
            gout[t] = new
            o32[pl.ds(t, GROUP, stride=frames), :] = new.astype(jnp.float32)
        part_out = gout.at[pl.ds(frames_of(b), CUTS[b])]
        pl.when(s < last)(lambda: spread(part_out, b, (s + 1) % sections, True, begin))

    def complete(b):
        return [k for k in (2, 1, 0) if k in range_of(b)]

    pl.when(s > 0)(prepare)
    for b in range(blocks):
        take(b)
        for t in range_of(b):
            build(g_own, x_own, t)

        @pl.when(s == last)
        def _():
            kernel_terms(b)
            for k in complete(b):
                sum_begin(k)

        if b < final:
            back_terms(b)
        else:
            pl.when(s < last)(lambda: back_terms(final))
        if b == min(1, final):
            pl.when(s == 0)(prepare)
        if b >= AHEAD - 1:
            if b < final:
                update(b - AHEAD + 1)
            else:
                pl.when(s < last)(lambda: update(final - AHEAD + 1))

    @pl.when(s < last)
    def _():
        for b in range(blocks - AHEAD + 1, blocks):
            update(b)
        grads_out()
        for b in range(blocks):
            kernel_terms(b)
            for k in complete(b):
                sum_begin(k)

    def between(k):
        @pl.when(s == last)
        def _():
            if k == 0:
                back_terms(final)
            if k == min(2, reach - 1):
                for b in range(final - AHEAD + 1, blocks):
                    update(b)
                grads_out()

    sum_finish(between)
    sum_sent()
    for p in range(3):
        out_copy(p).wait()
    grads_copy().wait()

    for q in range(chips):
        weight_copy(q).wait_send()

    @pl.when(s == 0)
    def _():
        for b in range(blocks):
            spread(block_of(g_own, b), b, s, False, sent)

    for b in range(blocks):
        per_slot(lambda slot: forward_copy(b, slot).wait_send())
        for o in hops:
            term_copy(b, (chip + o) % chips).wait_send()

    pl.when(s < sections - 1)(
        lambda: [
            spread(gout.at[pl.ds(frames_of(b), CUTS[b])], b, (s + 1) % sections, True, sent) for b in range(blocks)
        ] and None
    )


def pipeline(sections, rows, chips, frames, upstream, acts, weights):
    channels = weights.shape[1]
    width = 128
    blocks = len(CUTS)
    bf16, f32 = jnp.bfloat16, jnp.float32
    dma = pltpu.SemaphoreType.DMA
    vmem = pl.BlockSpec(memory_space=pltpu.VMEM)
    depth = (frames + 2) * SLAB + GROUP
    reach = rows // 4
    return pl.pallas_call(
        functools.partial(pipeline_kernel, sections, rows, chips, frames),
        out_shape=(
            jax.ShapeDtypeStruct((GROUP * frames, width), bf16),
            jax.ShapeDtypeStruct((27, 2, 2, 16, channels), bf16),
        ),
        in_specs=[vmem] * 3,
        out_specs=(pl.BlockSpec(memory_space=pl.ANY),) * 2,
        scratch_shapes=[
            pltpu.VMEM((3, frames + 2, GROUP, width), bf16),
            pltpu.VMEM((3, frames + 2, GROUP, width), bf16),
            pltpu.VMEM((depth, width), bf16),
            pltpu.VMEM((depth, width), bf16),
            pltpu.VMEM((2 * chips, GROUP, PADDED), bf16),
            pltpu.VMEM((chips, GROUP, PADDED), bf16),
            pltpu.VMEM((frames, chips, GROUP, width), bf16),
            pltpu.VMEM((frames, chips, GROUP, width), bf16),
            pltpu.VMEM((channels * frames, width), f32),
            pltpu.VMEM((frames, GROUP, width), f32),
            pltpu.VMEM((frames * width, channels), bf16),
            pltpu.VMEM((DEPTH, channels), f32),
            pltpu.VMEM((GROUP * frames, width), f32),
            pltpu.VMEM((frames, GROUP, width), bf16),
            pltpu.VMEM((27, 2, 2, 16, channels), bf16),
            pltpu.VMEM((27, 2, 2, 16, channels), bf16),
            pltpu.VMEM((3, 2, reach, 2, 9, 16, width), bf16),
            pltpu.VMEM((2, reach, 9, 16, width), bf16),
            pltpu.VMEM((3, 2, 2, 9, 16, width), bf16),
            pltpu.VMEM((3, 9, 16, width), bf16),
            pltpu.VMEM((9, 2, 16, channels), bf16),
            pltpu.VMEM((GROUP * frames, width), bf16),
            dma((blocks, 3)),
            dma((blocks, 3)),
            dma((blocks, 3)),
            dma((blocks, 3)),
            dma((blocks, 3)),
            dma((blocks, chips)),
            dma((blocks, chips)),
            dma((chips,)),
            dma((chips,)),
            dma((3, 2, reach)),
            dma((3, 2, reach)),
            dma((3,)),
            dma((3,)),
            dma((3, 2, reach, 2)),
            dma((3, 2, reach, 2)),
            dma((3,)),
            dma((3,)),
            dma((rows // 2,)),
            dma((rows // 2,)),
            dma((3, 2, 2)),
            dma((3, 2, 2)),
            dma((4,)),
        ],
        compiler_params=pltpu.CompilerParams(collective_id=0, has_side_effects=True),
        name="pipeline",
    )(upstream, acts, weights)


def hand_over_kernel(grads_in, wg_in, grads_ref, wg_ref, g_held, w_held, in_sem, out_sem):
    def steps(copy):
        for n in range(9):
            taps = pl.ds(3 * n, 3)
            copy(n, wg_in.at[taps], w_held.at[taps], wg_ref.at[taps])
        copy(9, grads_in, g_held, grads_ref)

    def fetch(n, source, held, target):
        pltpu.make_async_copy(source, held, in_sem.at[n]).start()

    def pass_on(n, source, held, target):
        pltpu.make_async_copy(source, held, in_sem.at[n]).wait()
        pltpu.make_async_copy(held, target, out_sem.at[n]).start()

    def finish(n, source, held, target):
        pltpu.make_async_copy(held, target, out_sem.at[n]).wait()

    steps(fetch)
    steps(pass_on)
    steps(finish)


def hand_over(grads, kernel_sum):
    anywhere = pl.BlockSpec(memory_space=pl.ANY)
    dma = pltpu.SemaphoreType.DMA
    return pl.pallas_call(
        hand_over_kernel,
        out_shape=tuple(jax.ShapeDtypeStruct(a.shape, a.dtype) for a in (grads, kernel_sum)),
        in_specs=[anywhere] * 2,
        out_specs=(anywhere,) * 2,
        scratch_shapes=[
            pltpu.VMEM(grads.shape, grads.dtype),
            pltpu.VMEM(kernel_sum.shape, kernel_sum.dtype),
            dma((10,)),
            dma((10,)),
        ],
        name="hand_over",
    )(grads, kernel_sum)


def solution(mesh):
    sections, rows, chans = (mesh.shape[a] for a in ("section", "frame", "chan"))

    def body(upstream, acts, weights):
        group, frames, _, width = upstream.shape
        channels = acts.shape[1]
        grads, kernel_sum = pipeline(
            sections,
            rows,
            chans // 2,
            frames,
            upstream.reshape(group * frames, width),
            acts.reshape(channels * frames, width),
            weights.reshape(27 * group, channels),
        )
        grads, kernel_sum = hand_over(grads, kernel_sum)
        return grads.reshape(1, group, frames, 1, width), kernel_sum.reshape(1, 27, group, channels)

    return jax.shard_map(
        body,
        mesh=mesh,
        in_specs=(
            P("chan", None, "frame", None),
            P("section", None, None, "frame", None),
            P("section", None, "chan", None),
        ),
        out_specs=(P("section", "chan", None, "frame", None), P("section", None, "chan", None)),
        check_vma=False,
    )
```
